256 devices in a mesh: cell: 64 (over z, x, y_lo), net: 4 (over y_hi, core).
Axes of the slice: x: 4, y: 4 (y_hi: 2, y_lo: 2; y = y_hi * 2 + y_lo), z: 8, core: 2. Of those that a mesh axis runs over, the one named last changes fastest.
Arguments:
- cell_feat: bfloat16 [32768, 256], P('cell'), may hold values from -6 to 6
- out_grad: bfloat16 [32768, 256], P('cell'), may hold values from -6 to 6
- w_in: bfloat16 [256, 1024], replicated, may hold values from -0.25 to 0.25
- w_net: bfloat16 [256, 1024], replicated, may hold values from -0.25 to 0.25
- bias: float32 [1024], replicated, may hold values from -3 to 3
- w_out: bfloat16 [1024, 256], replicated, may hold values from -0.1875 to 0.1875
- send_idx: int32 [64, 64, 16], P('cell'), may hold values from 0 to 511
- pin_net: int32 [64, 4, 2, 512], P('cell', 'net'), may hold values from 0 to 127
- pin_ref: int32 [64, 4, 2, 512], P('cell', 'net'), may hold values from 0 to 1535
- block_count: int32 [64, 4], P('cell', 'net'), may hold values from 1 to 2, as said below
Outputs:
- updated: bfloat16 [32768, 256], P(('cell', 'net'))
- cell_grad: bfloat16 [32768, 256], P(('cell', 'net'))
- grad_in: float32 [256, 1024], replicated
- grad_net: float32 [256, 1024], replicated
- grad_bias: float32 [1024], replicated
- grad_out: float32 [1024, 256], replicated
The draws below stay inside these ranges and needn't reach their ends.
Inputs may be any that keep to these rules, and one draw needn't show every extreme that they name: `block_count`: in each partition exactly one device of the net axis holds 2 live blocks; the others hold exactly 1.
All inputs are finite; a program needn't handle non-finite values.
Results may differ from the reference program's by a relative error of at most 0.0034.
Values may be sent and summed in bfloat16 or wider, within the bound.
A program may use at most 64 MiB of HBM per device.

```python
import jax
import jax.numpy as jnp
from jax import lax

F = 256
H = 1024
NETS_BLK = 128
P_BLK = 512
NB_MAX = 2
CELL_DEV = 512
SLOTS = 16
PARTITIONS = 64
NET_DEVS = 4
CELLS = 32768
TABLE = 1536


def draw_block_count(key, part):
    light_load = jax.random.randint(jax.random.fold_in(key, 11), (PARTITIONS, NET_DEVS), 1, NB_MAX // 2 + 1)
    heavy_at = jax.random.randint(jax.random.fold_in(key, 12), (PARTITIONS,), 0, NET_DEVS)
    column = jnp.arange(NET_DEVS, dtype=jnp.int32)
    return jnp.where(column[None, :] == heavy_at[:, None], NB_MAX, light_load).astype(jnp.int32)


def set_ends(drawn, key, least, high):
    spot = [jax.random.randint(jax.random.fold_in(key, axis), (), 0, length) for axis, length in enumerate(drawn.shape)]
    widest = drawn.shape.index(max(drawn.shape))
    beside = spot[:widest] + [(spot[widest] + 1) % drawn.shape[widest]] + spot[widest + 1:]
    return drawn.at[tuple(spot)].set(least).at[tuple(beside)].set(high)


def shard_levels(key, dims, shards, low, largest):
    loudness, own = 1.0, jax.random.fold_in(key, 6)
    for axis_at, shards_of in shards:
        draws = jnp.exp(jax.random.uniform(jax.random.fold_in(own, axis_at), (shards_of,), jnp.float32, low / len(shards), largest / len(shards)))
        loudness = loudness * jnp.repeat(draws, dims[axis_at] // shards_of).reshape([-1 if axis == axis_at else 1 for axis in range(len(dims))])
    return loudness


def gaussian(rng, extent, spread, most, split=(), kind=jnp.bfloat16):
    values = spread * jax.random.normal(rng, extent, jnp.float32)
    if split:
        values = values * shard_levels(rng, extent, split, -0.22, 0.18)
    return jnp.clip(values, -most, most).astype(kind)


def setup_inputs(seed: int = 0) -> dict:
    key_of = jax.random.split(jax.random.key(seed), 11)
    cell_feat = gaussian(key_of[0], (CELLS, F), 1.0, 6.0, ((0, 64),))
    out_grad = gaussian(key_of[1], (CELLS, F), 1.0, 6.0, ((0, 64),))
    w_in = gaussian(key_of[2], (F, H), (2 * F) ** -0.5, 0.25)
    w_net = gaussian(key_of[3], (F, H), (2 * F) ** -0.5, 0.25)
    bias = gaussian(key_of[4], (H,), 0.5, 3.0, (), jnp.float32)
    w_out = gaussian(key_of[5], (H, F), H ** -0.5, 0.1875)
    send_idx = set_ends(jax.random.randint(key_of[6], (PARTITIONS, PARTITIONS, SLOTS), 0, CELL_DEV), jax.random.fold_in(key_of[6], 1), 0, CELL_DEV - 1).astype(jnp.int32)
    pin_net = set_ends(jax.random.randint(key_of[7], (PARTITIONS, NET_DEVS, NB_MAX, P_BLK), 0, NETS_BLK), jax.random.fold_in(key_of[7], 1), 0, NETS_BLK - 1).astype(jnp.int32)
    pin_ref = set_ends(jax.random.randint(key_of[8], (PARTITIONS, NET_DEVS, NB_MAX, P_BLK), 0, TABLE), jax.random.fold_in(key_of[8], 1), 0, TABLE - 1).astype(jnp.int32)
    block_count = draw_block_count(jax.random.fold_in(key_of[10], 71), 0)
    return {"cell_feat": cell_feat, "out_grad": out_grad, "w_in": w_in, "w_net": w_net, "bias": bias, "w_out": w_out, "send_idx": send_idx, "pin_net": pin_net, "pin_ref": pin_ref, "block_count": block_count}


def block_pass(table_x, table_g, net_ids, refs, w_in, w_net, bias, w_out):
    pin_feat = table_x[refs]
    pin_grad = table_g[refs]
    onehot = (net_ids[:, None] == jnp.arange(NETS_BLK, dtype=jnp.int32)[None, :]).astype(jnp.bfloat16)
    counts = lax.optimization_barrier(jnp.sum(onehot.astype(jnp.float32), axis=0))
    inverse = 1.0 / jnp.maximum(counts, 1.0)
    net_sum = lax.dot_general(onehot, pin_feat, (((0,), (0,)), ((), ())), preferred_element_type=jnp.float32)
    net_feat = (net_sum * inverse[:, None]).astype(jnp.bfloat16)
    net_pre = jnp.dot(net_feat, w_net, preferred_element_type=jnp.float32).astype(jnp.bfloat16)
    pre_act = jnp.dot(pin_feat, w_in, preferred_element_type=jnp.float32) + jnp.dot(onehot, net_pre, preferred_element_type=jnp.float32) + bias
    hidden_full, gelu_back = jax.vjp(jax.nn.gelu, pre_act)
    hidden = hidden_full.astype(jnp.bfloat16)
    message = jnp.dot(hidden, w_out, preferred_element_type=jnp.float32)
    pulled = lax.dot_general(pin_grad, w_out, (((1,), (1,)), ((), ())), preferred_element_type=jnp.float32)
    pre_grad = gelu_back(pulled)[0].astype(jnp.bfloat16)
    grad_out = lax.dot_general(hidden, pin_grad, (((0,), (0,)), ((), ())), preferred_element_type=jnp.float32)
    grad_in = lax.dot_general(pin_feat, pre_grad, (((0,), (0,)), ((), ())), preferred_element_type=jnp.float32)
    grad_bias = lax.optimization_barrier(jnp.sum(pre_grad.astype(jnp.float32), axis=0))
    net_grad = lax.dot_general(onehot, pre_grad, (((0,), (0,)), ((), ())), preferred_element_type=jnp.float32).astype(jnp.bfloat16)
    grad_net = lax.dot_general(net_feat, net_grad, (((0,), (0,)), ((), ())), preferred_element_type=jnp.float32)
    feat_grad = (lax.dot_general(net_grad, w_net, (((1,), (1,)), ((), ())), preferred_element_type=jnp.float32) * inverse[:, None]).astype(jnp.bfloat16)
    pin_back = lax.dot_general(pre_grad, w_in, (((1,), (1,)), ((), ())), preferred_element_type=jnp.float32) + jnp.dot(onehot, feat_grad, preferred_element_type=jnp.float32)
    return (message, pin_back, (grad_in, grad_net, grad_bias, grad_out))

def reference(cell_feat, out_grad, w_in, w_net, bias, w_out, send_idx, pin_net, pin_ref, block_count):
    feat_dim = cell_feat.shape[1]
    hidden_dim = w_in.shape[1]
    grads_zero = (jnp.zeros((feat_dim, hidden_dim), jnp.float32), jnp.zeros((feat_dim, hidden_dim), jnp.float32), jnp.zeros((hidden_dim,), jnp.float32), jnp.zeros((hidden_dim, feat_dim), jnp.float32))
    initial = (jnp.zeros(cell_feat.shape, jnp.float32), jnp.zeros(cell_feat.shape, jnp.float32), grads_zero)

    def partition(part_no, running):
        acc_y, acc_x, gradients = running
        halo_rows = (jnp.arange(PARTITIONS, dtype=jnp.int32)[:, None] * CELL_DEV + send_idx[:, part_no, :].astype(jnp.int32)).reshape(-1).astype(jnp.int32)
        own_rows = (part_no * CELL_DEV + jnp.arange(CELL_DEV, dtype=jnp.int32)).astype(jnp.int32)
        table_rows = jnp.concatenate([own_rows, halo_rows])
        table_x = cell_feat[table_rows]
        table_g = out_grad[table_rows]
        local = (jnp.zeros((TABLE, feat_dim), jnp.float32), jnp.zeros((TABLE, feat_dim), jnp.float32), gradients)
        for net_no in range(NET_DEVS):

            def single_block(block_no, inner):
                local_y, local_x, grads_now = inner
                refs = pin_ref[part_no, net_no, block_no]
                message, pin_back, terms = block_pass(table_x, table_g, pin_net[part_no, net_no, block_no], refs, w_in, w_net, bias, w_out)
                return (local_y.at[refs].add(message), local_x.at[refs].add(pin_back), jax.tree.map(jnp.add, grads_now, terms))
            local = lax.fori_loop(0, block_count[part_no, net_no], single_block, local)
        return (acc_y.at[table_rows].add(local[0]), acc_x.at[table_rows].add(local[1]), local[2])
    acc_y, acc_x, gradients = lax.fori_loop(0, PARTITIONS, partition, initial)
    updated = (cell_feat.astype(jnp.float32) + acc_y).astype(jnp.bfloat16)
    cell_grad = (out_grad.astype(jnp.float32) + acc_x).astype(jnp.bfloat16)
    return (updated, cell_grad, gradients[0], gradients[1], gradients[2], gradients[3])
```

```python
import functools

import jax
import jax.numpy as jnp
from jax import lax
from jax.experimental import pallas as pl
from jax.experimental.pallas import tpu as pltpu
from jax.sharding import PartitionSpec as P

MESH = pl.DeviceIdType.MESH
NETS = 128
F = 256
HB = 256
VM = pl.BlockSpec(memory_space=pltpu.VMEM)
BF = jnp.bfloat16
F32 = jnp.float32
Z_SIZE = 8


def dot(a, b, ca, cb):
    return lax.dot_general(a, b, (((ca,), (cb,)), ((), ())), preferred_element_type=F32)


def place():
    c = lax.axis_index("cell")
    n = lax.axis_index("net")
    core = lax.rem(n, 2)
    return c, n, core, n // 2, n + 1 - 2 * core, lax.rem(n + 2, 4)


def send(src, dst, sems, dev):
    copy = pltpu.make_async_remote_copy(
        src_ref=src, dst_ref=dst, send_sem=sems[0], recv_sem=sems[1], device_id=dev, device_id_type=MESH
    )
    copy.start()


def arrived(ref, sems, dev):
    pltpu.make_async_remote_copy(
        src_ref=ref, dst_ref=ref, send_sem=sems[0], recv_sem=sems[1], device_id=dev, device_id_type=MESH
    ).wait_recv()


def left(ref, sems, dev):
    pltpu.make_async_remote_copy(
        src_ref=ref, dst_ref=ref, send_sem=sems[0], recv_sem=sems[1], device_id=dev, device_id_type=MESH
    ).wait_send()


def hail(barrier, dev):
    pl.semaphore_signal(barrier, inc=1, device_id=dev, device_id_type=MESH)


def row_select(idx_row, rows):
    return (lax.broadcasted_iota(jnp.int32, (rows, idx_row.shape[1]), 0) == idx_row).astype(F32).astype(BF)


def halo_kernel(nc, slots, x_ref, g_ref, idx_ref, net_ref, ref_ref, cnt_ref, halo_ref, eid_ref,
                send_buf, ids_buf, ids_recv, send_sem, recv_sem):
    c, n, core, y_hi, mate, across = place()
    barrier = pltpu.get_barrier_semaphore()

    def greet(k, _):
        hail(barrier, (lax.rem(c + k, nc), n))
        return 0

    lax.fori_loop(1, nc, greet, 0)
    for m in range(1, 4):
        hail(barrier, (c, lax.rem(n + m, 4)))

    live = (cnt_ref[...] == 2).astype(jnp.int32)
    ids_buf[...] = jnp.zeros_like(ids_buf)
    ids_buf[0:1, :] = ref_ref[1:2, :] * live
    ids_buf[1:2, :] = net_ref[1:2, :] * live
    table = jnp.where(core == 0, x_ref[...].astype(F32), g_ref[...].astype(F32)).astype(BF)
    rows = x_ref.shape[0]
    send_buf[...] = dot(row_select(idx_ref[...], rows), table, 0, 0).astype(BF)
    mine = pl.ds(pl.multiple_of(c * slots, slots), slots)
    halo_ref[core, mine, :] = send_buf[mine, :]
    ids_recv[n] = ids_buf[...]

    pl.semaphore_wait(barrier, nc - 1 + 3)

    s_ids = (send_sem.at[0], recv_sem.at[0])
    s_a2a = (send_sem.at[1], recv_sem.at[1])
    s_mate = (send_sem.at[2], recv_sem.at[2])
    for m in range(1, 4):
        send(ids_buf, ids_recv.at[n], s_ids, (c, lax.rem(n + m, 4)))

    def push(k, _):
        d = lax.rem(c + k, nc)
        send(send_buf.at[pl.ds(pl.multiple_of(d * slots, slots), slots)], halo_ref.at[core, mine], s_a2a, (d, n))
        return 0

    lax.fori_loop(1, nc, push, 0)
    most = pl.ds(0, (nc - 1) * slots)
    arrived(halo_ref.at[core, most], s_a2a, (c, mate))
    send(halo_ref.at[core], halo_ref.at[core], s_mate, (c, mate))
    arrived(ids_recv.at[pl.ds(0, 3)], s_ids, (c, mate))
    eid_ref[...] = ids_recv[0] + ids_recv[1] + ids_recv[2] + ids_recv[3]
    arrived(halo_ref.at[core], s_mate, (c, mate))
    left(ids_recv.at[pl.ds(0, 3)], s_ids, (c, mate))
    left(halo_ref.at[core, most], s_a2a, (c, mate))
    left(halo_ref.at[core], s_mate, (c, mate))


def gelu_pair(x):
    k = 0.7978845608028654
    sq = x * x
    t = jnp.tanh(k * (x + 0.044715 * (sq * x)))
    half = 0.5 * (1.0 + t)
    slope = half + (0.5 * k) * x * (1.0 - t * t) * (1.0 + 3.0 * 0.044715 * sq)
    return x * half, slope


def block_kernel(x_ref, g_ref, halo_ref, net_ref, ref_ref, eid_ref, w_in_ref, w_net_ref, bias_ref, w_out_ref,
                 own_ref, back_ref, grad_ref, pin_x, pin_g, pin_xt, scat, into, onto, net_feat, net_feat_t, inv,
                 msg, pback, facc, bsum):
    n = lax.axis_index("net")
    cells = x_ref.shape[0]
    outer = halo_ref.shape[1]
    pins = ref_ref.shape[1]
    for b in range(2):
        refs = ref_ref[0:1, :] if b == 0 else eid_ref[0:1, :]
        nets = net_ref[0:1, :] if b == 0 else eid_ref[1:2, :]
        scat[b] = row_select(refs, cells + outer)
        near = scat[b, 0:cells, :]
        far = scat[b, cells:, :]
        px = (dot(near, x_ref[...], 0, 0) + dot(far, halo_ref[0], 0, 0)).astype(BF)
        pg = (dot(near, g_ref[...], 0, 0) + dot(far, halo_ref[1], 0, 0)).astype(BF)
        pin_x[b] = px
        pin_g[b] = pg
        pin_xt[b] = px.astype(F32).T.astype(BF)
        hit = (lax.broadcasted_iota(jnp.int32, (NETS, pins), 0) == nets).astype(F32)
        into[b] = hit.astype(BF)
        onto[b] = hit.T.astype(BF)
        inv_b = 1.0 / jnp.maximum(jnp.sum(hit, axis=1, keepdims=True), 1.0)
        inv[b] = jnp.broadcast_to(inv_b, (NETS, F))
        nf = dot(hit.astype(BF), px, 1, 0) * inv_b
        nf = nf.astype(BF)
        net_feat[b] = nf
        net_feat_t[b] = nf.astype(F32).T.astype(BF)
    msg[...] = jnp.zeros_like(msg)
    pback[...] = jnp.zeros_like(pback)
    facc[...] = jnp.zeros_like(facc)
    grad_ref[...] = jnp.zeros_like(grad_ref)
    bsum[...] = jnp.zeros_like(bsum)

    def item(i, _):
        b = i // 4
        hb = jnp.where(i < 4, i, n)
        cols = pl.ds(pl.multiple_of(hb * HB, HB), HB)
        w_in = w_in_ref[:, cols]
        w_net = w_net_ref[:, cols]
        w_out = w_out_ref[cols, :]
        px = pin_x[b]
        pg = pin_g[b]
        net_pre = dot(net_feat[b], w_net, 1, 0).astype(BF)
        pre_act = dot(px, w_in, 1, 0) + dot(onto[b], net_pre, 1, 0) + bias_ref[:, cols]
        act, slope = gelu_pair(pre_act)
        hidden = act.astype(BF)
        msg[b] += dot(hidden, w_out, 1, 0)
        pre_grad = (dot(pg, w_out, 1, 1) * slope).astype(BF)
        net_grad = dot(into[b], pre_grad, 1, 0).astype(BF)
        pback[b] += dot(pre_grad, w_in, 1, 1)
        facc[b] += dot(net_grad, w_net, 1, 1)
        g_in = dot(pin_xt[b], pre_grad, 1, 0)
        g_net = dot(net_feat_t[b], net_grad, 1, 0)
        g_out = dot(hidden, pg, 0, 0)
        for h in range(2):
            part = slice(h * 128, h * 128 + 128)
            grad_ref[h, hb] += g_in[:, part]
            grad_ref[h, 4 + hb] += g_net[:, part]
            grad_ref[h, 8 + hb] += g_out[:, part]
        bias_row = jnp.sum(pre_grad.astype(F32), axis=0, keepdims=True)
        mark = lax.broadcasted_iota(jnp.int32, (16, HB), 0) == hb
        bsum[...] += jnp.where(mark, bias_row, 0.0)
        return 0

    lax.fori_loop(0, 5, item, 0)
    for h in range(2):
        for k in range(16):
            grad_ref[h, 12, k * 16 : k * 16 + 16, :] = bsum[:, h * 128 : h * 128 + 128]
    for b in range(2):
        feat_grad = (facc[b] * inv[b]).astype(BF)
        pback[b] += dot(onto[b], feat_grad, 1, 0)
    for k, vals in enumerate((msg, pback)):
        for b in range(2):
            v = vals[b]
            high = v.astype(BF)
            low = (v - high.astype(F32)).astype(BF)
            near = dot(scat[b, 0:cells, :], high, 1, 0) + dot(scat[b, 0:cells, :], low, 1, 0)
            far = dot(scat[b, cells:, :], high, 1, 0) + dot(scat[b, cells:, :], low, 1, 0)
            if b == 0:
                own_ref[k] = near
                back_ref[k] = far
            else:
                own_ref[k] += near
                back_ref[k] += far


def return_kernel(nc, zs, slots, x_ref, g_ref, idx_ref, own_ref, back_ref, grad_ref, out_ref, gout_ref, bout_ref,
                  halo_in, own_in, grad_in, a2a_buf, a2a_in, half_buf, half_in, fin, g_send, g_recv, z_send, z_recv,
                  z_fin, z_all, g_fin, b_fin, send_sem, recv_sem):
    c, n, core, y_hi, mate, across = place()
    xy = nc // zs
    peers = 2 * xy
    gr = 256 // peers
    zr = 12 * gr // zs
    z = c // xy
    base = z * xy
    p = lax.rem(c, xy) * 2 + y_hi
    barrier = pltpu.get_barrier_semaphore()
    sem = lambda i: (send_sem.at[i], recv_sem.at[i])
    near = (c, mate)

    def greet(k, _):
        hail(barrier, (lax.rem(c + k, nc), n))
        return 0

    def greet_across(k, _):
        hail(barrier, (base + k, across))
        return 0

    lax.fori_loop(1, nc, greet, 0)
    lax.fori_loop(0, xy, greet_across, 0)
    hail(barrier, near)
    pl.semaphore_wait(barrier, nc - 1 + xy + 1)

    other = 1 - core
    send(back_ref.at[other], halo_in, sem(0), near)
    send(own_ref.at[other], own_in, sem(1), near)
    send(grad_ref.at[other], grad_in, sem(2), near)

    arrived(halo_in, sem(0), near)
    a2a_buf[...] = (back_ref[core] + halo_in[...]).astype(BF)
    mine = pl.ds(pl.multiple_of(c * slots, slots), slots)

    def push(k, _):
        d = lax.rem(c + k, nc)
        send(a2a_buf.at[pl.ds(pl.multiple_of(d * slots, slots), slots)], a2a_in.at[mine], sem(3), (d, n))
        return 0

    lax.fori_loop(1, nc, push, 0)
    a2a_in[mine, :] = a2a_buf[mine, :]

    arrived(grad_in, sem(2), near)
    g_send[...] = (grad_ref[core] + grad_in[...]).astype(BF)

    def push_xy(k, _):
        t = lax.rem(p + k, peers)
        rows = pl.ds(pl.multiple_of(t * gr, gr), gr)
        send(g_send.at[:, rows, :], g_recv.at[p], sem(4), (base + t // 2, lax.rem(t, 2) * 2 + core))
        return 0

    lax.fori_loop(1, peers, push_xy, 0)
    g_rows = pl.ds(pl.multiple_of(p * gr, gr), gr)
    g_recv[p] = g_send[:, g_rows, :]
    arrived(own_in, sem(1), near)
    half_all = own_ref[core] + own_in[...]

    arrived(g_recv.at[pl.ds(0, peers - 1)], sem(4), near)
    total = g_recv[0].astype(F32)
    for k in range(1, peers):
        total += g_recv[k].astype(F32)
    flat = total.reshape(13 * gr, 128)
    for k in range(zs):
        z_send[k, 0:zr, :] = flat[k * zr : k * zr + zr, :]
        z_send[k, zr : zr + 8, :] = flat[12 * gr : 12 * gr + 8, :]

    def push_z(k, _):
        t = lax.rem(z + k, zs)
        send(z_send.at[t], z_recv.at[z], sem(5), (t * xy + lax.rem(c, xy), n))
        return 0

    lax.fori_loop(1, zs, push_z, 0)
    z_recv[z] = z_send[z]

    most = pl.ds(0, (nc - 1) * slots)
    arrived(a2a_in.at[most], sem(3), near)
    rows = x_ref.shape[0]
    half_buf[...] = half_all + dot(row_select(idx_ref[...], rows), a2a_in[...], 1, 0)
    hr = rows // 2
    there = pl.ds(pl.multiple_of((1 - y_hi) * hr, hr), hr)
    here = pl.ds(pl.multiple_of(y_hi * hr, hr), hr)
    send(half_buf.at[there], half_in, sem(6), (c, across))

    arrived(z_recv.at[pl.ds(0, zs - 1)], sem(5), near)
    zsum = z_recv[0]
    for k in range(1, zs):
        zsum += z_recv[k]
    z_fin[...] = zsum[0:zr, :]
    b_fin[...] = zsum[zr : zr + 8, :]

    def push_zg(k, _):
        t = lax.rem(z + k, zs)
        send(z_fin, z_all.at[z], sem(7), (t * xy + lax.rem(c, xy), n))
        return 0

    lax.fori_loop(1, zs, push_zg, 0)
    z_all[z] = z_fin[...]
    bout_ref[core] = b_fin[...]
    send(b_fin, bout_ref.at[core], sem(8), near)

    arrived(half_in, sem(6), near)
    seed = jnp.where(core == 0, x_ref[here, :].astype(F32), g_ref[here, :].astype(F32))
    fin[...] = (half_buf[here, :] + half_in[...] + seed).astype(BF)
    qr = hr // 2
    theirs = pl.ds(pl.multiple_of((1 - core) * qr, qr), qr)
    ours = pl.ds(pl.multiple_of(core * qr, qr), qr)
    send(fin.at[theirs], out_ref.at[core], sem(9), near)
    out_ref[core] = fin[ours, :]

    arrived(z_all.at[pl.ds(0, zs - 1)], sem(7), near)
    g_fin[...] = z_all[...].reshape(12, gr, 128).astype(BF)

    def push_g(k, _):
        t = lax.rem(p + k, peers)
        send(g_fin, gout_ref.at[core, :, g_rows, :], sem(10), (base + t // 2, lax.rem(t, 2) * 2 + core))
        return 0

    lax.fori_loop(1, peers, push_g, 0)
    gout_ref[core, :, g_rows, :] = g_fin[...]
    arrived(g_recv.at[pl.ds(0, peers - 1), pl.ds(0, 12)], sem(10), near)
    send(gout_ref.at[core], gout_ref.at[core], sem(11), near)
    arrived(b_fin, sem(8), near)
    arrived(fin.at[ours], sem(9), near)
    arrived(gout_ref.at[core], sem(11), near)

    left(halo_in, sem(0), near)
    left(own_in, sem(1), near)
    left(grad_in, sem(2), near)
    left(a2a_in.at[most], sem(3), near)
    left(g_recv.at[pl.ds(0, peers - 1)], sem(4), near)
    left(z_recv.at[pl.ds(0, zs - 1)], sem(5), near)
    left(half_in, sem(6), near)
    left(z_all.at[pl.ds(0, zs - 1)], sem(7), near)
    left(b_fin, sem(8), near)
    left(fin.at[ours], sem(9), near)
    left(g_recv.at[pl.ds(0, peers - 1), pl.ds(0, 12)], sem(10), near)
    left(gout_ref.at[core], sem(11), near)


def shape(dims, kind):
    return jax.ShapeDtypeStruct(dims, kind)


def local(nc, zs, cell_feat, out_grad, w_in, w_net, bias, w_out, send_idx, pin_net, pin_ref, block_count):
    rows = cell_feat.shape[0]
    slots = send_idx.shape[2]
    outer = nc * slots
    pins = pin_ref.shape[3]
    hidden = w_in.shape[1]
    idx = send_idx.reshape(1, outer)
    nets = pin_net.reshape(2, pins)
    refs = pin_ref.reshape(2, pins)
    peers = 2 * nc // zs
    gr = 256 // peers
    zr = 12 * gr // zs
    dma = pltpu.SemaphoreType.DMA

    halo, eids = pl.pallas_call(
        functools.partial(halo_kernel, nc, slots),
        out_shape=(shape((2, outer, F), BF), shape((8, pins), jnp.int32)),
        in_specs=[VM] * 6,
        out_specs=(VM, VM),
        scratch_shapes=[
            pltpu.VMEM((outer, F), BF),
            pltpu.VMEM((8, pins), jnp.int32),
            pltpu.VMEM((4, 8, pins), jnp.int32),
            dma((3,)),
            dma((3,)),
        ],
        compiler_params=pltpu.CompilerParams(collective_id=0, has_side_effects=True),
        name="halo",
    )(cell_feat, out_grad, idx, nets, refs, block_count)

    own, back, grads = pl.pallas_call(
        block_kernel,
        out_shape=(shape((2, rows, F), F32), shape((2, outer, F), F32), shape((2, 13, 256, 128), F32)),
        in_specs=[VM] * 10,
        out_specs=(VM, VM, VM),
        scratch_shapes=[
            pltpu.VMEM((2, pins, F), BF),
            pltpu.VMEM((2, pins, F), BF),
            pltpu.VMEM((2, F, pins), BF),
            pltpu.VMEM((2, rows + outer, pins), BF),
            pltpu.VMEM((2, NETS, pins), BF),
            pltpu.VMEM((2, pins, NETS), BF),
            pltpu.VMEM((2, NETS, F), BF),
            pltpu.VMEM((2, F, NETS), BF),
            pltpu.VMEM((2, NETS, F), F32),
            pltpu.VMEM((2, pins, F), F32),
            pltpu.VMEM((2, pins, F), F32),
            pltpu.VMEM((2, NETS, F), F32),
            pltpu.VMEM((16, HB), F32),
        ],
        name="blocks",
    )(cell_feat, out_grad, halo, nets, refs, eids, w_in, w_net, bias.reshape(1, hidden), w_out)

    outs, gout, bout = pl.pallas_call(
        functools.partial(return_kernel, nc, zs, slots),
        out_shape=(shape((2, rows // 4, F), BF), shape((2, 12, 256, 128), BF), shape((2, 8, 128), F32)),
        in_specs=[VM] * 6,
        out_specs=(VM, VM, VM),
        scratch_shapes=[
            pltpu.VMEM((outer, F), F32),
            pltpu.VMEM((rows, F), F32),
            pltpu.VMEM((13, 256, 128), F32),
            pltpu.VMEM((outer, F), BF),
            pltpu.VMEM((outer, F), BF),
            pltpu.VMEM((rows, F), F32),
            pltpu.VMEM((rows // 2, F), F32),
            pltpu.VMEM((rows // 2, F), BF),
            pltpu.VMEM((13, 256, 128), BF),
            pltpu.VMEM((peers, 13, gr, 128), BF),
            pltpu.VMEM((zs, zr + 8, 128), F32),
            pltpu.VMEM((zs, zr + 8, 128), F32),
            pltpu.VMEM((zr, 128), F32),
            pltpu.VMEM((zs, zr, 128), F32),
            pltpu.VMEM((12, gr, 128), BF),
            pltpu.VMEM((8, 128), F32),
            dma((12,)),
            dma((12,)),
        ],
        compiler_params=pltpu.CompilerParams(collective_id=1, has_side_effects=True),
        name="back",
    )(cell_feat, out_grad, idx, own, back, grads)

    def whole(t):
        return gout[:, 4 * t : 4 * t + 4].transpose(2, 1, 0, 3).reshape(F, hidden).astype(F32)

    grad_out = gout[:, 8:12].transpose(1, 2, 0, 3).reshape(hidden, F).astype(F32)
    grad_bias = bout[:, 0:4].transpose(1, 0, 2).reshape(hidden)
    return (outs[0], outs[1], whole(0), whole(1), grad_bias, grad_out)


def solution(mesh):
    nc = mesh.shape["cell"]
    placed = (
        P("cell", None), P("cell", None), P(), P(), P(), P(),
        P("cell", None, None), P("cell", "net", None, None), P("cell", "net", None, None), P("cell", "net"),
    )
    return jax.shard_map(
        functools.partial(local, nc, Z_SIZE),
        mesh=mesh,
        in_specs=placed,
        out_specs=(P(("cell", "net"), None), P(("cell", "net"), None), P(), P(), P(), P()),
        check_vma=False,
    )
```

```python
import functools

import jax
import jax.numpy as jnp
from jax import lax
from jax.experimental import pallas as pl
from jax.experimental.pallas import tpu as pltpu
from jax.sharding import PartitionSpec as P

MESH = pl.DeviceIdType.MESH
NETS = 128
F = 256
HB = 256
VM = pl.BlockSpec(memory_space=pltpu.VMEM)
ANY = pl.BlockSpec(memory_space=pl.ANY)
BF = jnp.bfloat16
F32 = jnp.float32
I32 = jnp.int32
Z_SIZE = 8


def dot(a, b, ca, cb):
    return lax.dot_general(a, b, (((ca,), (cb,)), ((), ())), preferred_element_type=F32)


def remote(src, dst, sems, dev):
    return pltpu.make_async_remote_copy(
        src_ref=src, dst_ref=dst, send_sem=sems[0], recv_sem=sems[1], device_id=dev, device_id_type=MESH
    )


def iota(dims, axis):
    return lax.broadcasted_iota(I32, dims, axis)


def ones_where(mask):
    return mask.astype(F32).astype(BF)


def gelu_pair(x):
    k = 0.7978845608028654
    sq = x * x
    t = jnp.tanh(k * (x + 0.044715 * (sq * x)))
    half = 0.5 * (1.0 + t)
    slope = half + (0.5 * k) * x * (1.0 - t * t) * (1.0 + 3.0 * 0.044715 * sq)
    return x * half, slope


def layer_kernel(nc, zs, slots,
                 x_ref, g_ref, idx_ref, net_ref, ref_ref, cnt_ref, w_in_hbm, w_net_hbm, bias_ref, w_out_hbm,
                 out_ref, gout_ref, bout_ref,
                 w_in_ref, w_net_ref, w_out_ref, send_buf, halo, ids_buf, ids_recv, sel_t, gath, scat, pin, pin_xt,
                 into, onto, net_feat, net_feat_t, inv, acc, facc, bsum, grads, grad_in, g_send, g_recv, b_in, b_send,
                 b_recv, far_buf, far_in, near_buf, near_in, a2a_buf, a2a_in, half_buf, half_in, fin,
                 z_send, z_recv, z_fin, z_all, g_fin, b_fin, w_sem, send_sem, recv_sem):
    c = lax.axis_index("cell")
    n = lax.axis_index("net")
    core = lax.rem(n, 2)
    other = 1 - core
    y_hi = n // 2
    mate = n + 1 - 2 * core
    across = lax.rem(n + 2, 4)
    xy = nc // zs
    peers = 2 * xy
    gr = 256 // peers
    zr = 12 * gr // zs
    z = c // xy
    base = z * xy
    p = lax.rem(c, xy) * 2 + y_hi
    near = (c, mate)
    cells = x_ref.shape[0]
    outer = nc * slots
    pins = ref_ref.shape[1]
    sem = lambda i: (send_sem.at[i], recv_sem.at[i])

    def send(src, dst, i, dev):
        remote(src, dst, sem(i), dev).start()

    def arrived(ref, i):
        remote(ref, ref, sem(i), near).wait_recv()

    def left(ref, i):
        remote(ref, ref, sem(i), near).wait_send()

    def xy_dev(t):
        return (base + t // 2, lax.rem(t, 2) * 2 + core)

    def rows_at(k, size):
        return pl.ds(pl.multiple_of(k * size, size), size)

    barrier = pltpu.get_barrier_semaphore()

    def hail(dev):
        pl.semaphore_signal(barrier, inc=1, device_id=dev, device_id_type=MESH)

    def greet(k, _):
        hail((lax.rem(c + k, nc), n))
        return 0

    def greet_across(k, _):
        hail((base + k, across))
        return 0

    lax.fori_loop(1, nc, greet, 0)
    lax.fori_loop(0, xy, greet_across, 0)
    hail(near)
    hail((c, 3 - n))

    loads = [
        pltpu.make_async_copy(src, dst, w_sem.at[i])
        for i, (src, dst) in enumerate(((w_in_hbm, w_in_ref), (w_net_hbm, w_net_ref), (w_out_hbm, w_out_ref)))
    ]
    for load in loads:
        load.start()

    idx = idx_ref[...]
    high = (idx // 2).astype(F32).astype(BF)
    low = lax.rem(idx, 2).astype(F32).astype(BF)
    pick = ones_where(iota((outer, nc), 0) // slots == iota((outer, nc), 1))
    spread = 2.0 * dot(pick, high, 1, 0) + dot(pick, low, 1, 0)
    keep = lax.rem(iota((outer, slots), 0), slots) == iota((outer, slots), 1)
    idx_col = jnp.sum(jnp.where(keep, spread, 0.0), axis=1, keepdims=True).astype(I32)
    table = jnp.where(core == 0, x_ref[...].astype(F32), g_ref[...].astype(F32)).astype(BF)
    send_buf[...] = dot(ones_where(iota((outer, cells), 1) == idx_col), table, 1, 0).astype(BF)
    live = (cnt_ref[...] == 2).astype(I32)
    ids_buf[...] = jnp.zeros_like(ids_buf)
    ids_buf[0:1, :] = ref_ref[1:2, :] * live
    ids_buf[1:2, :] = net_ref[1:2, :] * live

    pl.semaphore_wait(barrier, nc - 1 + xy + 2)

    mine = rows_at(c, slots)

    def push(k, _):
        d = lax.rem(c + k, nc)
        send(send_buf.at[rows_at(d, slots)], halo.at[core, mine], 0, (d, n))
        return 0

    lax.fori_loop(1, nc, push, 0)
    for m in range(1, 4):
        send(ids_buf, ids_recv.at[n], 1, (c, lax.rem(n + m, 4)))
    halo[core, mine, :] = send_buf[mine, :]
    ids_recv[n] = ids_buf[...]

    def lists(b, refs, nets):
        ids = jnp.concatenate([refs, nets, jnp.zeros((6, pins), I32)], axis=0).astype(F32)
        cols = ids.T.astype(I32)
        gath[b] = ones_where(iota((pins, cells + outer), 1) == cols[:, 0:1])
        scat[:, b * pins : (b + 1) * pins] = ones_where(iota((cells + outer, pins), 0) == refs)
        hit = (iota((NETS, pins), 0) == nets).astype(F32)
        into[b] = hit.astype(BF)
        onto[b] = ones_where(iota((pins, NETS), 1) == cols[:, 1:2])
        inv[b] = jnp.broadcast_to(1.0 / jnp.maximum(jnp.sum(hit, axis=1, keepdims=True), 1.0), (NETS, F))
        pin[0, b] = dot(gath[b, :, 0:cells], x_ref[...], 1, 0).astype(BF)
        pin[1, b] = dot(gath[b, :, 0:cells], g_ref[...], 1, 0).astype(BF)

    lists(0, ref_ref[0:1, :], net_ref[0:1, :])
    grads[...] = jnp.zeros_like(grads)
    acc[...] = jnp.zeros_like(acc)
    bsum[...] = jnp.zeros_like(bsum)
    facc[...] = jnp.zeros_like(facc)
    arrived(ids_recv.at[pl.ds(0, 3)], 1)
    ids = ids_recv[0] + ids_recv[1] + ids_recv[2] + ids_recv[3]
    lists(1, ids[0:1, :], ids[1:2, :])
    idx_row = jnp.broadcast_to(idx_col.astype(F32), (outer, 8)).T[0:1, :].astype(I32)
    sel_t[...] = ones_where(iota((cells, outer), 0) == idx_row)
    for load in loads:
        load.wait()

    most = pl.ds(0, (nc - 1) * slots)
    arrived(halo.at[core, most], 0)
    send(halo.at[core], halo.at[core], 2, near)

    def fetch(k):
        for b in range(2):
            pin[k, b] += dot(gath[b, :, cells:], halo[k], 1, 0).astype(BF)

    fetch(core)
    arrived(halo.at[core], 2)
    fetch(other)

    for b in range(2):
        px = pin[0, b]
        pin_xt[b] = px.astype(F32).T.astype(BF)
        nf = (dot(into[b], px, 1, 0) * inv[b]).astype(BF)
        net_feat[b] = nf
        net_feat_t[b] = nf.astype(F32).T.astype(BF)

    def item(b, hb):
        cols = rows_at(hb, HB)
        w_in = w_in_ref[:, cols]
        w_net = w_net_ref[:, cols]
        w_out = w_out_ref[cols, :]
        px = pin[0, b]
        pg = pin[1, b]
        net_pre = dot(net_feat[b], w_net, 1, 0).astype(BF)
        pre_act = dot(px, w_in, 1, 0) + dot(onto[b], net_pre, 1, 0) + bias_ref[:, cols]
        act, slope = gelu_pair(pre_act)
        hidden = act.astype(BF)
        acc[0, b] += dot(hidden, w_out, 1, 0)
        pre_grad = (dot(pg, w_out, 1, 1) * slope).astype(BF)
        net_grad = dot(into[b], pre_grad, 1, 0).astype(BF)
        acc[1, b] += dot(pre_grad, w_in, 1, 1)
        facc[b] += dot(net_grad, w_net, 1, 1)
        terms = (
            dot(pin_xt[b], pre_grad, 1, 0),
            dot(net_feat_t[b], net_grad, 1, 0),
            dot(hidden, pg, 0, 0),
        )
        for h in range(2):
            for t in range(3):
                grads[h, hb * 3 + t] += terms[t][:, h * 128 : h * 128 + 128]
        bias_row = jnp.sum(pre_grad.astype(F32), axis=0, keepdims=True)
        for h in range(2):
            bsum[h] += jnp.where(iota((16, 128), 0) == hb, bias_row[:, h * 128 : h * 128 + 128], 0.0)

    g_rows = rows_at(p, gr)

    def spread_grads(hb):
        part = pl.ds(hb * 3, 3)
        arrived(grad_in.at[part], 3 + hb)
        g_send[part] = (grads[core, part] + grad_in[part]).astype(BF)

        def push_xy(k, _):
            t = lax.rem(p + k, peers)
            send(g_send.at[part, rows_at(t, gr), :], g_recv.at[hb, p], 7 + hb, xy_dev(t))
            return 0

        lax.fori_loop(1, peers, push_xy, 0)
        g_recv[hb, p] = g_send[part, g_rows, :]

    item(1, n)

    def turn(hb, _):
        item(0, hb)
        part = pl.ds(hb * 3, 3)
        send(grads.at[other, part], grad_in.at[part], 3 + hb, near)

        @pl.when(hb > 0)
        def _():
            spread_grads(hb - 1)

        return 0

    lax.fori_loop(0, 4, turn, 0)
    send(bsum.at[other], b_in, 11, near)
    for b in range(2):
        feat_grad = (facc[b] * inv[b]).astype(BF)
        acc[1, b] += dot(onto[b], feat_grad, 1, 0)

    def scatter(k):
        vals = acc[k].reshape(2 * pins, F)
        high = vals.astype(BF)
        low = (vals - high.astype(F32)).astype(BF)
        out = scat[cells:, :]
        far_buf[k] = dot(out, high, 1, 0) + dot(out, low, 1, 0)
        out = scat[0:cells, :]
        near_buf[k] = dot(out, high, 1, 0) + dot(out, low, 1, 0)

    scatter(other)
    send(far_buf.at[other], far_in, 12, near)
    send(near_buf.at[other], near_in, 13, near)
    spread_grads(3)
    arrived(b_in, 11)
    b_send[...] = (bsum[core] + b_in[...]).astype(BF)

    def push_b(k, _):
        t = lax.rem(p + k, peers)
        send(b_send, b_recv.at[p], 14, xy_dev(t))
        return 0

    lax.fori_loop(1, peers, push_b, 0)
    b_recv[p] = b_send[...]
    scatter(core)
    arrived(far_in, 12)
    a2a_buf[...] = (far_buf[core] + far_in[...]).astype(BF)

    def push_back(k, _):
        d = lax.rem(c + k, nc)
        send(a2a_buf.at[rows_at(d, slots)], a2a_in.at[mine], 15, (d, n))
        return 0

    lax.fori_loop(1, nc, push_back, 0)
    a2a_in[mine, :] = a2a_buf[mine, :]

    arrived(near_in, 13)
    half_buf[...] = near_buf[core] + near_in[...]

    part_sums = []
    for hb in range(4):
        arrived(g_recv.at[hb, pl.ds(0, peers - 1)], 7 + hb)
        total = g_recv[hb, 0].astype(F32)
        for k in range(1, peers):
            total += g_recv[hb, k].astype(F32)
        part_sums.append(total.reshape(3 * gr, 128))
    flat = jnp.concatenate(part_sums, axis=0)
    arrived(b_recv.at[pl.ds(0, peers - 1)], 14)
    b_sum = b_recv[0].astype(F32)
    for k in range(1, peers):
        b_sum += b_recv[k].astype(F32)
    for k in range(zs):
        z_send[k, 0:zr, :] = flat[k * zr : k * zr + zr, :]
        z_send[k, zr : zr + 8, :] = b_sum[0:8, :]

    def z_dev(t):
        return (t * xy + lax.rem(c, xy), n)

    def push_z(k, _):
        t = lax.rem(z + k, zs)
        send(z_send.at[t], z_recv.at[z], 16, z_dev(t))
        return 0

    lax.fori_loop(1, zs, push_z, 0)
    z_recv[z] = z_send[z]
    arrived(z_recv.at[pl.ds(0, zs - 1)], 16)
    zsum = z_recv[0]
    for k in range(1, zs):
        zsum += z_recv[k]
    z_fin[...] = zsum[0:zr, :]
    b_fin[...] = zsum[zr : zr + 8, :]

    def push_zg(k, _):
        t = lax.rem(z + k, zs)
        send(z_fin, z_all.at[z], 17, z_dev(t))
        return 0

    lax.fori_loop(1, zs, push_zg, 0)
    z_all[z] = z_fin[...]
    bout_ref[core] = b_fin[...]
    send(b_fin, bout_ref.at[core], 18, near)

    arrived(a2a_in.at[most], 15)
    half_buf[...] += dot(sel_t[...], a2a_in[...], 1, 0)
    hr = cells // 2
    here = rows_at(y_hi, hr)
    send(half_buf.at[rows_at(1 - y_hi, hr)], half_in, 19, (c, across))

    arrived(z_all.at[pl.ds(0, zs - 1)], 17)
    g_fin[...] = z_all[...].reshape(12, gr, 128).astype(BF)

    def push_g(k, _):
        t = lax.rem(p + k, peers)
        send(g_fin, gout_ref.at[core, :, g_rows, :], 20, xy_dev(t))
        return 0

    lax.fori_loop(1, peers, push_g, 0)
    gout_ref[core, :, g_rows, :] = g_fin[...]

    arrived(half_in, 19)
    seed = jnp.where(core == 0, x_ref[here, :].astype(F32), g_ref[here, :].astype(F32))
    fin[...] = (half_buf[here, :] + half_in[...] + seed).astype(BF)
    qr = hr // 2
    ours = rows_at(core, qr)
    send(fin.at[rows_at(other, qr)], out_ref.at[core], 21, near)
    out_ref[core] = fin[ours, :]

    every = g_recv.at[pl.ds(0, 4), pl.ds(0, peers - 1)]
    arrived(every, 20)
    send(gout_ref.at[core], gout_ref.at[core], 22, near)
    arrived(b_fin, 18)
    arrived(fin.at[ours], 21)

    left(halo.at[core, most], 0)
    left(ids_recv.at[pl.ds(0, 3)], 1)
    left(halo.at[core], 2)
    for hb in range(4):
        left(grad_in.at[pl.ds(hb * 3, 3)], 3 + hb)
        left(g_recv.at[hb, pl.ds(0, peers - 1)], 7 + hb)
    left(b_in, 11)
    left(far_in, 12)
    left(near_in, 13)
    left(b_recv.at[pl.ds(0, peers - 1)], 14)
    left(a2a_in.at[most], 15)
    left(z_recv.at[pl.ds(0, zs - 1)], 16)
    left(z_all.at[pl.ds(0, zs - 1)], 17)
    left(b_fin, 18)
    left(half_in, 19)
    left(every, 20)
    left(fin.at[ours], 21)
    arrived(gout_ref.at[core], 22)
    left(gout_ref.at[core], 22)


def finish_kernel(outs_ref, gout_ref, bout_ref, y_ref, x_ref, gin_ref, gnet_ref, gbias_ref, gout_full):
    y_ref[...] = outs_ref[0]
    x_ref[...] = outs_ref[1]
    for hb in range(4):
        for h in range(2):
            cols = slice(hb * 256 + h * 128, hb * 256 + h * 128 + 128)
            gin_ref[:, cols] = gout_ref[h, hb * 3].astype(F32)
            gnet_ref[:, cols] = gout_ref[h, hb * 3 + 1].astype(F32)
            gout_full[hb * 256 : hb * 256 + 256, h * 128 : h * 128 + 128] = gout_ref[h, hb * 3 + 2].astype(F32)
            gbias_ref[:, cols] = bout_ref[h, hb : hb + 1, :]


def shape(dims, kind):
    return jax.ShapeDtypeStruct(dims, kind)


def local(nc, zs, cell_feat, out_grad, w_in, w_net, bias, w_out, send_idx, pin_net, pin_ref, block_count):
    rows = cell_feat.shape[0]
    slots = send_idx.shape[2]
    outer = nc * slots
    pins = pin_ref.shape[3]
    hidden = w_in.shape[1]
    peers = 2 * nc // zs
    gr = 256 // peers
    zr = 12 * gr // zs
    dma = pltpu.SemaphoreType.DMA
    vm = pltpu.VMEM

    outs, gout, bout = pl.pallas_call(
        functools.partial(layer_kernel, nc, zs, slots),
        out_shape=(shape((2, rows // 4, F), BF), shape((2, 12, 256, 128), BF), shape((2, 8, 128), F32)),
        in_specs=[VM] * 6 + [ANY, ANY, VM, ANY],
        out_specs=(VM, VM, VM),
        scratch_shapes=[
            vm((F, hidden), BF),
            vm((F, hidden), BF),
            vm((hidden, F), BF),
            vm((outer, F), BF),
            vm((2, outer, F), BF),
            vm((8, pins), I32),
            vm((4, 8, pins), I32),
            vm((rows, outer), BF),
            vm((2, pins, rows + outer), BF),
            vm((rows + outer, 2 * pins), BF),
            vm((2, 2, pins, F), BF),
            vm((2, F, pins), BF),
            vm((2, NETS, pins), BF),
            vm((2, pins, NETS), BF),
            vm((2, NETS, F), BF),
            vm((2, F, NETS), BF),
            vm((2, NETS, F), F32),
            vm((2, 2, pins, F), F32),
            vm((2, NETS, F), F32),
            vm((2, 16, 128), F32),
            vm((2, 12, 256, 128), F32),
            vm((12, 256, 128), F32),
            vm((12, 256, 128), BF),
            vm((4, peers, 3, gr, 128), BF),
            vm((16, 128), F32),
            vm((16, 128), BF),
            vm((peers, 16, 128), BF),
            vm((2, outer, F), F32),
            vm((outer, F), F32),
            vm((2, rows, F), F32),
            vm((rows, F), F32),
            vm((outer, F), BF),
            vm((outer, F), BF),
            vm((rows, F), F32),
            vm((rows // 2, F), F32),
            vm((rows // 2, F), BF),
            vm((zs, zr + 8, 128), F32),
            vm((zs, zr + 8, 128), F32),
            vm((zr, 128), F32),
            vm((zs, zr, 128), F32),
            vm((12, gr, 128), BF),
            vm((8, 128), F32),
            dma((3,)),
            dma((23,)),
            dma((23,)),
        ],
        compiler_params=pltpu.CompilerParams(collective_id=0, has_side_effects=True),
        name="layer",
    )(cell_feat, out_grad, send_idx.reshape(nc, slots), pin_net.reshape(2, pins), pin_ref.reshape(2, pins),
      block_count, w_in, w_net, bias.reshape(1, hidden), w_out)

    updated, cell_grad, grad_in, grad_net, grad_bias, grad_out = pl.pallas_call(
        finish_kernel,
        out_shape=(
            shape((rows // 4, F), BF), shape((rows // 4, F), BF), shape((F, hidden), F32),
            shape((F, hidden), F32), shape((1, hidden), F32), shape((hidden, F), F32),
        ),
        in_specs=[VM] * 3,
        out_specs=(VM,) * 6,
        name="finish",
    )(outs, gout, bout)
    return (updated, cell_grad, grad_in, grad_net, grad_bias.reshape(hidden), grad_out)


def solution(mesh):
    nc = mesh.shape["cell"]
    placed = (
        P("cell", None), P("cell", None), P(), P(), P(), P(),
        P("cell", None, None), P("cell", "net", None, None), P("cell", "net", None, None), P("cell", "net"),
    )
    return jax.shard_map(
        functools.partial(local, nc, Z_SIZE),
        mesh=mesh,
        in_specs=placed,
        out_specs=(P(("cell", "net"), None), P(("cell", "net"), None), P(), P(), P(), P()),
        check_vma=False,
    )
```

```python
import functools

import jax
import jax.numpy as jnp
from jax import lax
from jax.experimental import pallas as pl
from jax.experimental.pallas import tpu as pltpu
from jax.sharding import PartitionSpec as P

MESH = pl.DeviceIdType.MESH
NETS = 128
F = 256
HB = 256
VM = pl.BlockSpec(memory_space=pltpu.VMEM)
ANY = pl.BlockSpec(memory_space=pl.ANY)
HBM = pl.BlockSpec(memory_space=pltpu.HBM)
BF = jnp.bfloat16
F32 = jnp.float32
I32 = jnp.int32
Z_SIZE = 8
WAVES = (2, 2)


def dot(a, b, ca, cb):
    return lax.dot_general(a, b, (((ca,), (cb,)), ((), ())), preferred_element_type=F32)


def remote(src, dst, sems, dev):
    return pltpu.make_async_remote_copy(
        src_ref=src, dst_ref=dst, send_sem=sems[0], recv_sem=sems[1], device_id=dev, device_id_type=MESH
    )


def iota(dims, axis):
    return lax.broadcasted_iota(I32, dims, axis)


def ones_where(mask):
    return mask.astype(F32).astype(BF)


def gelu_pair(x):
    k = 0.7978845608028654
    q = k * 0.044715
    sq = x * x
    half = 0.5 + 0.5 * jnp.tanh(x * (k + q * sq))
    act = x * half
    return act, half + (act - act * half) * (2.0 * k + 6.0 * q * sq)


def layer_kernel(nc, zs, slots,
                 x_ref, g_ref, idx_ref, net_ref, ref_ref, cnt_ref, w_in_hbm, w_net_hbm, bias_ref, w_out_hbm,
                 out_ref, gout_ref, gz_ref, bout_ref,
                 w_in_ref, w_net_ref, w_out_ref, send_buf, halo, ids_buf, ids_recv, sel_t, gath, scat, pin, pin_xt,
                 into, onto, net_feat, net_feat_t, inv, hid, slope_g, net_g, vals, bsum, grads, grad_in, g_send, g_recv,
                 b_in, b_send, b_recv, far_buf, far_in, near_buf, near_in, a2a_buf, a2a_in, half_buf, half_in, fin,
                 z_send, z_recv, z_fin, z_all, g_fin, b_fin, q_recv, r_send, r_recv, gz_fin, w_sem, send_sem, recv_sem):
    c = lax.axis_index("cell")
    n = lax.axis_index("net")
    core = lax.rem(n, 2)
    other = 1 - core
    y_hi = n // 2
    mate = n + 1 - 2 * core
    across = lax.rem(n + 2, 4)
    xy = nc // zs
    peers = 2 * xy
    gr = 256 // peers
    zr = 8 * gr // zs
    zq = 256 // zs
    zz = 4 * zq // peers
    z = c // xy
    base = z * xy
    p = lax.rem(c, xy) * 2 + y_hi
    near = (c, mate)
    cells = x_ref.shape[0]
    outer = nc * slots
    pins = ref_ref.shape[1]
    sem = lambda i: (send_sem.at[i], recv_sem.at[i])

    def send(src, dst, i, dev):
        remote(src, dst, sem(i), dev).start()

    def arrived(ref, i):
        remote(ref, ref, sem(i), near).wait_recv()

    def left(ref, i):
        remote(ref, ref, sem(i), near).wait_send()

    def xy_dev(t):
        return (base + t // 2, lax.rem(t, 2) * 2 + core)

    def z_dev(t):
        return (t * xy + lax.rem(c, xy), n)

    def rows_at(k, size):
        return pl.ds(pl.multiple_of(k * size, size), size)

    barrier = pltpu.get_barrier_semaphore()

    def hail(dev):
        pl.semaphore_signal(barrier, inc=1, device_id=dev, device_id_type=MESH)

    def greet(k, _):
        hail((lax.rem(c + k, nc), n))
        return 0

    def greet_across(k, _):
        hail((base + k, across))
        return 0

    lax.fori_loop(1, nc, greet, 0)
    lax.fori_loop(0, xy, greet_across, 0)
    hail(near)
    hail((c, 3 - n))

    loads = [
        pltpu.make_async_copy(src, dst, w_sem.at[i])
        for i, (src, dst) in enumerate(((w_in_hbm, w_in_ref), (w_net_hbm, w_net_ref), (w_out_hbm, w_out_ref)))
    ]
    for load in loads:
        load.start()

    idx = idx_ref[...]
    high = (idx // 2).astype(F32).astype(BF)
    low = lax.rem(idx, 2).astype(F32).astype(BF)
    pick = ones_where(iota((outer, nc), 0) // slots == iota((outer, nc), 1))
    spread = 2.0 * dot(pick, high, 1, 1) + dot(pick, low, 1, 1)
    keep = lax.rem(iota((outer, slots), 0), slots) == iota((outer, slots), 1)
    idx_col = jnp.sum(jnp.where(keep, spread, 0.0), axis=1, keepdims=True).astype(I32)
    table = jnp.where(core == 0, x_ref[...].astype(F32), g_ref[...].astype(F32)).astype(BF)
    send_buf[...] = dot(ones_where(iota((outer, cells), 1) == idx_col), table, 1, 0).astype(BF)
    live = (cnt_ref[...] == 2).astype(I32)
    ids_buf[...] = jnp.zeros_like(ids_buf)
    ids_buf[0:1, :] = ref_ref[1:2, :] * live
    ids_buf[1:2, :] = net_ref[1:2, :] * live

    pl.semaphore_wait(barrier, nc - 1 + xy + 2)

    mine = rows_at(c, slots)

    def push(k, _):
        d = lax.rem(c + k, nc)
        send(send_buf.at[rows_at(d, slots)], halo.at[core, mine], 0, (d, n))
        return 0

    lax.fori_loop(1, nc, push, 0)
    for m in range(1, 4):
        send(ids_buf, ids_recv.at[n], 1, (c, lax.rem(n + m, 4)))
    halo[core, mine, :] = send_buf[mine, :]
    ids_recv[n] = ids_buf[...]

    def lists(b, refs, nets):
        ids = jnp.concatenate([refs, nets, jnp.zeros((6, pins), I32)], axis=0).astype(F32)
        cols = ids.T.astype(I32)
        gath[b] = ones_where(iota((pins, cells + outer), 1) == cols[:, 0:1])
        scat[:, b * pins : (b + 1) * pins] = ones_where(iota((cells + outer, pins), 0) == refs)
        hit = (iota((NETS, pins), 0) == nets).astype(F32)
        into[b] = hit.astype(BF)
        onto[b] = ones_where(iota((pins, NETS), 1) == cols[:, 1:2])
        inv[b] = jnp.broadcast_to(1.0 / jnp.maximum(jnp.sum(hit, axis=1, keepdims=True), 1.0), (NETS, F))
        pin[0, b] = dot(gath[b, :, 0:cells], x_ref[...], 1, 0).astype(BF)
        pin[1, b] = dot(gath[b, :, 0:cells], g_ref[...], 1, 0).astype(BF)

    lists(0, ref_ref[0:1, :], net_ref[0:1, :])
    grads[...] = jnp.zeros_like(grads)
    bsum[...] = jnp.zeros_like(bsum)
    arrived(ids_recv.at[pl.ds(0, 3)], 1)
    ids = ids_recv[0] + ids_recv[1] + ids_recv[2] + ids_recv[3]
    lists(1, ids[0:1, :], ids[1:2, :])
    idx_row = jnp.broadcast_to(idx_col.astype(F32), (outer, 8)).T[0:1, :].astype(I32)
    sel_t[...] = ones_where(iota((cells, outer), 0) == idx_row)
    for load in loads:
        load.wait()

    most = pl.ds(0, (nc - 1) * slots)
    arrived(halo.at[core, most], 0)
    send(halo.at[core], halo.at[core], 2, near)

    def fetch(k):
        for b in range(2):
            pin[k, b] += dot(gath[b, :, cells:], halo[k], 1, 0).astype(BF)

    fetch(core)
    arrived(halo.at[core], 2)
    fetch(other)

    for b in range(2):
        px = pin[0, b]
        pin_xt[b] = px.astype(F32).T.astype(BF)
        nf = (dot(into[b], px, 1, 0) * inv[b]).astype(BF)
        net_feat[b] = nf
        net_feat_t[b] = nf.astype(F32).T.astype(BF)

    def item(b, hb, slot):
        cols = rows_at(hb, HB)
        place = rows_at(slot, HB)
        w_in = w_in_ref[:, cols]
        w_net = w_net_ref[:, cols]
        w_out = w_out_ref[cols, :]
        px = pin[0, b]
        pg = pin[1, b]
        net_pre = dot(net_feat[b], w_net, 1, 0).astype(BF)
        pre_act = dot(px, w_in, 1, 0) + dot(onto[b], net_pre, 1, 0) + bias_ref[:, cols]
        act, slope = gelu_pair(pre_act)
        hidden = act.astype(BF)
        hid[:, place] = hidden
        pre_grad = (dot(pg, w_out, 1, 1) * slope).astype(BF)
        net_grad = dot(into[b], pre_grad, 1, 0).astype(BF)
        slope_g[:, place] = pre_grad
        net_g[:, place] = net_grad
        terms = (
            dot(pin_xt[b], pre_grad, 1, 0),
            dot(hidden, pg, 0, 0),
            dot(net_feat_t[b], net_grad, 1, 0),
        )
        for h in range(2):
            for t in range(3):
                grads[h, hb * 3 + t] += terms[t][:, h * 128 : h * 128 + 128]
        bias_row = jnp.sum(pre_grad.astype(F32), axis=0, keepdims=True)
        for h in range(2):
            bsum[h] += jnp.where(iota((16, 128), 0) == hb, bias_row[:, h * 128 : h * 128 + 128], 0.0)

    g_rows = rows_at(p, gr)

    def spread_grads(hb):
        part = pl.ds(hb * 3, 3)
        arrived(grad_in.at[part], 3 + hb)
        g_send[part] = (grads[core, part] + grad_in[part]).astype(BF)

        pair = pl.ds(hb * 3, 2)

        def push_xy(k, _):
            t = lax.rem(p + k, peers)
            send(g_send.at[pair, rows_at(t, gr), :], g_recv.at[hb, p], 7 + hb, xy_dev(t))
            return 0

        def push_q(k, _):
            t = lax.rem(z + k, zs)
            send(g_send.at[hb * 3 + 2, rows_at(t, zq), :], q_recv.at[hb, z], 25 + hb, z_dev(t))
            return 0

        lax.fori_loop(1, peers, push_xy, 0)
        lax.fori_loop(1, zs, push_q, 0)
        g_recv[hb, p] = g_send[pair, g_rows, :]
        q_recv[hb, z] = g_send[hb * 3 + 2, rows_at(z, zq), :]

    item(1, n, 4)

    def turn(hb, _):
        item(0, hb, hb)
        part = pl.ds(hb * 3, 3)
        send(grads.at[other, part], grad_in.at[part], 3 + hb, near)

        @pl.when(hb > 0)
        def _():
            spread_grads(hb - 1)

        return 0

    lax.fori_loop(0, 4, turn, 0)
    send(bsum.at[other], b_in, 11, near)
    wide = 4 * HB
    extra = rows_at(n, HB)
    pairs = (
        (slice(0, wide), w_in_ref[...], w_net_ref[...], w_out_ref[...]),
        (slice(wide, wide + HB), w_in_ref[:, extra], w_net_ref[:, extra], w_out_ref[extra, :]),
    )
    backs = []
    for b, (cols, w_in, w_net, w_out) in enumerate(pairs):
        mine_b = slice(b * pins, (b + 1) * pins)
        vals[0, mine_b, :] = dot(hid[:, cols], w_out, 1, 0).astype(BF)
        feat_grad = (dot(net_g[:, cols], w_net, 1, 1) * inv[b]).astype(BF)
        vals[1, mine_b, :] = (dot(slope_g[:, cols], w_in, 1, 1) + dot(onto[b], feat_grad, 1, 0)).astype(BF)
    spread_grads(3)

    def scatter(k):
        far_buf[k] = dot(scat[cells:, :], vals[k], 1, 0)
        near_buf[k] = dot(scat[0:cells, :], vals[k], 1, 0)

    scatter(other)
    send(far_buf.at[other], far_in, 12, near)
    send(near_buf.at[other], near_in, 13, near)
    arrived(b_in, 11)
    b_send[...] = (bsum[core] + b_in[...]).astype(BF)

    def push_b(k, _):
        t = lax.rem(p + k, peers)
        send(b_send, b_recv.at[p], 14, xy_dev(t))
        return 0

    lax.fori_loop(1, peers, push_b, 0)
    b_recv[p] = b_send[...]
    scatter(core)

    arrived(far_in, 12)
    a2a_buf[...] = (far_buf[core] + far_in[...]).astype(BF)

    def push_back(k, _):
        d = lax.rem(c + k, nc)
        send(a2a_buf.at[rows_at(d, slots)], a2a_in.at[mine], 15, (d, n))
        return 0

    first = 1 + (nc - 1) * WAVES[0] // 8
    second = first + (nc - 1) * WAVES[1] // 8
    lax.fori_loop(1, first, push_back, 0)
    a2a_in[mine, :] = a2a_buf[mine, :]
    arrived(near_in, 13)
    half_buf[...] = near_buf[core] + near_in[...]

    part_sums = []
    for hb in range(4):
        arrived(g_recv.at[hb, pl.ds(0, peers - 1)], 7 + hb)
        total = g_recv[hb, 0].astype(F32)
        for k in range(1, peers):
            total += g_recv[hb, k].astype(F32)
        part_sums.append(total.reshape(2 * gr, 128))
    flat = jnp.concatenate(part_sums, axis=0)
    arrived(b_recv.at[pl.ds(0, peers - 1)], 14)
    b_sum = b_recv[0].astype(F32)
    for k in range(1, peers):
        b_sum += b_recv[k].astype(F32)
    for k in range(zs):
        z_send[k, 0:zr, :] = flat[k * zr : k * zr + zr, :]
        z_send[k, zr : zr + 8, :] = b_sum[0:8, :]

    def push_z(k, _):
        t = lax.rem(z + k, zs)
        send(z_send.at[t], z_recv.at[z], 16, z_dev(t))
        return 0

    lax.fori_loop(1, zs, push_z, 0)

    lax.fori_loop(first, second, push_back, 0)
    z_recv[z] = z_send[z]

    q_sums = []
    for hb in range(4):
        arrived(q_recv.at[hb, pl.ds(0, zs - 1)], 25 + hb)
        total = q_recv[hb, 0].astype(F32)
        for k in range(1, zs):
            total += q_recv[hb, k].astype(F32)
        q_sums.append(total)
    r_send[...] = jnp.concatenate(q_sums, axis=0).reshape(peers, zz, 128)

    def push_r(k, _):
        t = lax.rem(p + k, peers)
        send(r_send.at[t], r_recv.at[p], 29, xy_dev(t))
        return 0

    lax.fori_loop(1, peers, push_r, 0)
    r_recv[p] = r_send[p]

    arrived(z_recv.at[pl.ds(0, zs - 1)], 16)
    zsum = z_recv[0]
    for k in range(1, zs):
        zsum += z_recv[k]
    z_fin[0:zr, :] = zsum[0:zr, :]
    b_fin[...] = zsum[zr : zr + 8, :]
    arrived(r_recv.at[pl.ds(0, peers - 1)], 29)
    rsum = r_recv[0]
    for k in range(1, peers):
        rsum += r_recv[k]
    z_fin[zr : zr + zz, :] = rsum

    def push_zg(k, _):
        t = lax.rem(z + k, zs)
        send(z_fin, z_all.at[z], 17, z_dev(t))
        return 0

    lax.fori_loop(1, zs, push_zg, 0)
    lax.fori_loop(second, nc, push_back, 0)
    z_all[z] = z_fin[...]
    bout_ref[core] = b_fin[...]
    send(b_fin, bout_ref.at[core], 18, near)

    arrived(z_all.at[pl.ds(0, zs - 1)], 17)
    g_fin[...] = z_all[:, 0:zr, :].reshape(8, gr, 128).astype(BF)
    gz_fin[...] = z_all[:, zr : zr + zz, :].reshape(zs * zz, 128).astype(BF)
    xn = peers // 4
    x_at = p // 4
    y_at = lax.rem(p, 4)
    one, two = pl.ds(0, 6), pl.ds(6, 2)

    def to_x(k):
        return xy_dev(lax.rem(x_at + k, xn) * 4 + y_at)

    def to_y(k):
        return xy_dev(x_at * 4 + lax.rem(y_at + k, 4))

    for k in range(1, xn):
        send(g_fin.at[one], gout_ref.at[core, one, x_at, y_at], 20, to_x(k))
    for k in range(1, 4):
        send(g_fin.at[two], gout_ref.at[core, two, x_at, y_at], 22, to_y(k))
        send(gz_fin, gz_ref.at[core, x_at, y_at], 30, to_y(k))
    gout_ref[core, :, x_at, y_at] = g_fin[...]
    gz_ref[core, x_at, y_at] = gz_fin[...]
    if xn > 1:
        arrived(gout_ref.at[core, one, pl.ds(0, xn - 1), 0], 20)
    for k in range(1, 4):
        send(gout_ref.at[core, one, :, y_at], gout_ref.at[core, one, :, y_at], 21, to_y(k))
    arrived(gout_ref.at[core, two, 0, pl.ds(0, 3)], 22)
    arrived(gz_ref.at[core, 0, pl.ds(0, 3)], 30)
    for k in range(1, xn):
        send(gout_ref.at[core, two, x_at], gout_ref.at[core, two, x_at], 23, to_x(k))
        send(gz_ref.at[core, x_at], gz_ref.at[core, x_at], 31, to_x(k))

    arrived(a2a_in.at[most], 15)
    half_buf[...] += dot(sel_t[...], a2a_in[...], 1, 0)
    fin[...] = half_buf[...].astype(BF)
    qr = cells // 4
    ours = rows_at(n, qr)
    for k, q in enumerate((mate, across, 3 - n)):
        send(fin.at[rows_at(q, qr)], half_in.at[k], 19, (c, q))
    arrived(half_in, 19)
    kept = half_buf[ours, :] + half_in[1].astype(F32)
    swapped = half_in[0].astype(F32) + half_in[2].astype(F32)
    as_x = jnp.where(core == 0, kept, swapped)
    as_g = jnp.where(core == 0, swapped, kept)
    out_ref[0] = (as_x + x_ref[ours, :].astype(F32)).astype(BF)
    out_ref[1] = (as_g + g_ref[ours, :].astype(F32)).astype(BF)

    arrived(gout_ref.at[core, one, :, pl.ds(0, 3)], 21)
    if xn > 1:
        arrived(gout_ref.at[core, two, pl.ds(0, xn - 1)], 23)
        arrived(gz_ref.at[core, pl.ds(0, xn - 1)], 31)
    send(gout_ref.at[core], gout_ref.at[core], 24, near)
    send(gz_ref.at[core], gz_ref.at[core], 32, near)
    arrived(b_fin, 18)

    left(halo.at[core, most], 0)
    left(ids_recv.at[pl.ds(0, 3)], 1)
    left(halo.at[core], 2)
    for hb in range(4):
        left(grad_in.at[pl.ds(hb * 3, 3)], 3 + hb)
        left(g_recv.at[hb, pl.ds(0, peers - 1)], 7 + hb)
        left(q_recv.at[hb, pl.ds(0, zs - 1)], 25 + hb)
    left(b_in, 11)
    left(far_in, 12)
    left(near_in, 13)
    left(b_recv.at[pl.ds(0, peers - 1)], 14)
    left(a2a_in.at[most], 15)
    left(z_recv.at[pl.ds(0, zs - 1)], 16)
    left(z_all.at[pl.ds(0, zs - 1)], 17)
    left(b_fin, 18)
    left(r_recv.at[pl.ds(0, peers - 1)], 29)
    left(gz_ref.at[core, 0, pl.ds(0, 3)], 30)
    left(half_in, 19)
    left(gout_ref.at[core, one, :, pl.ds(0, 3)], 21)
    left(gout_ref.at[core, two, 0, pl.ds(0, 3)], 22)
    if xn > 1:
        left(gout_ref.at[core, one, pl.ds(0, xn - 1), 0], 20)
        left(gout_ref.at[core, two, pl.ds(0, xn - 1)], 23)
        left(gz_ref.at[core, pl.ds(0, xn - 1)], 31)
    arrived(gout_ref.at[core], 24)
    left(gout_ref.at[core], 24)
    arrived(gz_ref.at[core], 32)
    left(gz_ref.at[core], 32)


def finish_kernel(zs, outs_ref, gout_ref, gz_ref, bout_ref, y_ref, x_ref, gin_ref, gnet_ref, gbias_ref, gout_full,
                  gin, gnet, gfull, gbias, sem):
    copies = []
    zq = 256 // zs
    zz = gz_ref.shape[2] // zs
    per = gz_ref.shape[1] // 4

    def put(src, dst):
        copies.append(pltpu.make_async_copy(src, dst, sem.at[len(copies)]))
        copies[-1].start()

    put(outs_ref.at[0], y_ref)
    put(outs_ref.at[1], x_ref)
    for hb in range(4):
        block = slice(hb * 256, hb * 256 + 256)
        for h in range(2):
            cols = slice(hb * 256 + h * 128, hb * 256 + h * 128 + 128)
            gin[:, cols] = gout_ref[h, hb * 2].astype(F32)
            gfull[block, h * 128 : h * 128 + 128] = gout_ref[h, hb * 2 + 1].astype(F32)
            for r in range(per):
                piece = gz_ref[h, hb * per + r].astype(F32)
                for z in range(zs):
                    at = z * zq + r * zz
                    gnet[at : at + zz, cols] = piece[z * zz : z * zz + zz]
            gbias[:, cols] = bout_ref[h, hb : hb + 1, :]
        put(gin.at[:, block], gin_ref.at[:, block])
        put(gnet.at[:, block], gnet_ref.at[:, block])
        put(gfull.at[block], gout_full.at[block])
    put(gbias, gbias_ref)
    for copy in copies:
        copy.wait()


def shape(dims, kind):
    return jax.ShapeDtypeStruct(dims, kind)


def local(nc, zs, cell_feat, out_grad, w_in, w_net, bias, w_out, send_idx, pin_net, pin_ref, block_count):
    rows = cell_feat.shape[0]
    slots = send_idx.shape[2]
    outer = nc * slots
    pins = pin_ref.shape[3]
    hidden = w_in.shape[1]
    peers = 2 * nc // zs
    gr = 256 // peers
    zr = 8 * gr // zs
    zq = 256 // zs
    zz = 4 * zq // peers
    dma = pltpu.SemaphoreType.DMA
    vm = pltpu.VMEM

    outs, gout, gz, bout = pl.pallas_call(
        functools.partial(layer_kernel, nc, zs, slots),
        out_shape=(shape((2, rows // 4, F), BF), shape((2, 8, peers // 4, 4, gr, 128), BF),
                   shape((2, peers // 4, 4, zs * zz, 128), BF), shape((2, 8, 128), F32)),
        in_specs=[VM] * 6 + [HBM, HBM, VM, HBM],
        out_specs=(VM,) * 4,
        scratch_shapes=[
            vm((F, hidden), BF),
            vm((F, hidden), BF),
            vm((hidden, F), BF),
            vm((outer, F), BF),
            vm((2, outer, F), BF),
            vm((8, pins), I32),
            vm((4, 8, pins), I32),
            vm((rows, outer), BF),
            vm((2, pins, rows + outer), BF),
            vm((rows + outer, 2 * pins), BF),
            vm((2, 2, pins, F), BF),
            vm((2, F, pins), BF),
            vm((2, NETS, pins), BF),
            vm((2, pins, NETS), BF),
            vm((2, NETS, F), BF),
            vm((2, F, NETS), BF),
            vm((2, NETS, F), F32),
            vm((pins, 5 * HB), BF),
            vm((pins, 5 * HB), BF),
            vm((NETS, 5 * HB), BF),
            vm((2, 2 * pins, F), BF),
            vm((2, 16, 128), F32),
            vm((2, 12, 256, 128), F32),
            vm((12, 256, 128), F32),
            vm((12, 256, 128), BF),
            vm((4, peers, 2, gr, 128), BF),
            vm((16, 128), F32),
            vm((16, 128), BF),
            vm((peers, 16, 128), BF),
            vm((2, outer, F), F32),
            vm((outer, F), F32),
            vm((2, rows, F), F32),
            vm((rows, F), F32),
            vm((outer, F), BF),
            vm((outer, F), BF),
            vm((rows, F), F32),
            vm((3, rows // 4, F), BF),
            vm((rows, F), BF),
            vm((zs, zr + 8, 128), F32),
            vm((zs, zr + 8, 128), F32),
            vm((zr + zz, 128), F32),
            vm((zs, zr + zz, 128), F32),
            vm((8, gr, 128), BF),
            vm((8, 128), F32),
            vm((4, zs, zq, 128), BF),
            vm((peers, zz, 128), F32),
            vm((peers, zz, 128), F32),
            vm((zs * zz, 128), BF),
            dma((3,)),
            dma((33,)),
            dma((33,)),
        ],
        compiler_params=pltpu.CompilerParams(collective_id=0, has_side_effects=True),
        name="layer",
    )(cell_feat, out_grad, send_idx[0].T, pin_net.reshape(2, pins), pin_ref.reshape(2, pins),
      block_count, w_in, w_net, bias.reshape(1, hidden), w_out)

    updated, cell_grad, grad_in, grad_net, grad_bias, grad_out = pl.pallas_call(
        functools.partial(finish_kernel, zs),
        out_shape=(
            shape((rows // 4, F), BF), shape((rows // 4, F), BF), shape((F, hidden), F32),
            shape((F, hidden), F32), shape((1, hidden), F32), shape((hidden, F), F32),
        ),
        in_specs=[VM] * 4,
        out_specs=(ANY,) * 6,
        scratch_shapes=[
            vm((F, hidden), F32), vm((F, hidden), F32), vm((hidden, F), F32), vm((1, hidden), F32), dma((15,)),
        ],
        name="finish",
    )(outs, gout.reshape(2, 8, 256, 128), gz.reshape(2, peers, zs * zz, 128), bout)
    return (updated, cell_grad, grad_in, grad_net, grad_bias.reshape(hidden), grad_out)


def solution(mesh):
    nc = mesh.shape["cell"]
    placed = (
        P("cell", None), P("cell", None), P(), P(), P(), P(),
        P("cell", None, None), P("cell", "net", None, None), P("cell", "net", None, None), P("cell", "net"),
    )
    return jax.shard_map(
        functools.partial(local, nc, Z_SIZE),
        mesh=mesh,
        in_specs=placed,
        out_specs=(P(("cell", "net"), None), P(("cell", "net"), None), P(), P(), P(), P()),
        check_vma=False,
    )
```

```python
import functools

import jax
import jax.numpy as jnp
from jax import lax
from jax.experimental import pallas as pl
from jax.experimental.pallas import tpu as pltpu
from jax.sharding import PartitionSpec as P

MESH = pl.DeviceIdType.MESH
NETS = 128
F = 256
HB = 256
VM = pl.BlockSpec(memory_space=pltpu.VMEM)
ANY = pl.BlockSpec(memory_space=pl.ANY)
HBM = pl.BlockSpec(memory_space=pltpu.HBM)
BF = jnp.bfloat16
F32 = jnp.float32
I32 = jnp.int32
Z_SIZE = 8
WAVE = 2


def dot(a, b, ca, cb):
    return lax.dot_general(a, b, (((ca,), (cb,)), ((), ())), preferred_element_type=F32)


def remote(src, dst, sems, dev):
    return pltpu.make_async_remote_copy(
        src_ref=src, dst_ref=dst, send_sem=sems[0], recv_sem=sems[1], device_id=dev, device_id_type=MESH
    )


def iota(dims, axis):
    return lax.broadcasted_iota(I32, dims, axis)


def ones_where(mask):
    return mask.astype(F32).astype(BF)


def gelu_pair(x):
    k = 0.7978845608028654
    q = k * 0.044715
    sq = x * x
    half = 0.5 + 0.5 * jnp.tanh(x * (k + q * sq))
    act = x * half
    return act, half + (act - act * half) * (2.0 * k + 6.0 * q * sq)


def layer_kernel(nc, zs, slots,
                 x_ref, g_ref, idx_ref, net_ref, ref_ref, cnt_ref, w_in_hbm, w_net_hbm, bias_ref, w_out_hbm,
                 out_ref, gout_ref, gz_ref, bout_ref,
                 w_in_ref, w_net_ref, w_out_ref, send_buf, halo, ids_buf, ids_recv, sel_t, gath, scat, pin, pin_xt,
                 into, onto, net_feat, net_feat_t, inv, hid, slope_g, net_g, vals, bsum, grads, grad_in, g_send, g_recv,
                 b_in, b_send, b_recv, far_buf, far_in, near_buf, near_in, a2a_buf, a2a_in, half_buf, half_in, fin,
                 z_send, z_recv, bz_send, bz_recv, g_fin, q_recv, r_send, r_recv, r_fin, r_all, gz_fin, w_sem, send_sem, recv_sem):
    c = lax.axis_index("cell")
    n = lax.axis_index("net")
    core = lax.rem(n, 2)
    other = 1 - core
    y_hi = n // 2
    mate = n + 1 - 2 * core
    across = lax.rem(n + 2, 4)
    xy = nc // zs
    peers = 2 * xy
    gr = 256 // peers
    zq = 256 // zs
    zz = 4 * zq // peers
    z = c // xy
    base = z * xy
    p = lax.rem(c, xy) * 2 + y_hi
    near = (c, mate)
    cells = x_ref.shape[0]
    outer = nc * slots
    pins = ref_ref.shape[1]
    sem = lambda i: (send_sem.at[i], recv_sem.at[i])

    def send(src, dst, i, dev):
        remote(src, dst, sem(i), dev).start()

    def arrived(ref, i):
        remote(ref, ref, sem(i), near).wait_recv()

    def left(ref, i):
        remote(ref, ref, sem(i), near).wait_send()

    def xy_dev(t):
        return (base + t // 2, lax.rem(t, 2) * 2 + core)

    def z_dev(t):
        return (t * xy + lax.rem(c, xy), n)

    def rows_at(k, size):
        return pl.ds(pl.multiple_of(k * size, size), size)

    barrier = pltpu.get_barrier_semaphore()

    def hail(dev):
        pl.semaphore_signal(barrier, inc=1, device_id=dev, device_id_type=MESH)

    def greet(k, _):
        hail((lax.rem(c + k, nc), n))
        return 0

    def greet_across(k, _):
        hail((base + k, across))
        return 0

    lax.fori_loop(1, nc, greet, 0)
    lax.fori_loop(0, xy, greet_across, 0)
    hail(near)
    hail((c, 3 - n))

    loads = [
        pltpu.make_async_copy(src, dst, w_sem.at[i])
        for i, (src, dst) in enumerate(((w_in_hbm, w_in_ref), (w_net_hbm, w_net_ref), (w_out_hbm, w_out_ref)))
    ]
    for load in loads:
        load.start()

    idx = idx_ref[...]
    high = (idx // 2).astype(F32).astype(BF)
    low = lax.rem(idx, 2).astype(F32).astype(BF)
    pick = ones_where(iota((outer, nc), 0) // slots == iota((outer, nc), 1))
    spread = 2.0 * dot(pick, high, 1, 1) + dot(pick, low, 1, 1)
    keep = lax.rem(iota((outer, slots), 0), slots) == iota((outer, slots), 1)
    idx_col = jnp.sum(jnp.where(keep, spread, 0.0), axis=1, keepdims=True).astype(I32)
    table = jnp.where(core == 0, x_ref[...].astype(F32), g_ref[...].astype(F32)).astype(BF)
    send_buf[...] = dot(ones_where(iota((outer, cells), 1) == idx_col), table, 1, 0).astype(BF)
    live = (cnt_ref[...] == 2).astype(I32)
    ids_buf[...] = jnp.zeros_like(ids_buf)
    ids_buf[0:1, :] = ref_ref[1:2, :] * live
    ids_buf[1:2, :] = net_ref[1:2, :] * live

    pl.semaphore_wait(barrier, nc - 1 + xy + 2)

    mine = rows_at(c, slots)

    def push(k, _):
        d = lax.rem(c + k, nc)
        send(send_buf.at[rows_at(d, slots)], halo.at[core, mine], 0, (d, n))
        return 0

    lax.fori_loop(1, nc, push, 0)
    for m in range(1, 4):
        send(ids_buf, ids_recv.at[n], 1, (c, lax.rem(n + m, 4)))
    halo[core, mine, :] = send_buf[mine, :]
    ids_recv[n] = ids_buf[...]

    def lists(b, refs, nets):
        ids = jnp.concatenate([refs, nets, jnp.zeros((6, pins), I32)], axis=0).astype(F32)
        cols = ids.T.astype(I32)
        gath[b] = ones_where(iota((pins, cells + outer), 1) == cols[:, 0:1])
        scat[:, b * pins : (b + 1) * pins] = ones_where(iota((cells + outer, pins), 0) == refs)
        hit = (iota((NETS, pins), 0) == nets).astype(F32)
        into[b] = hit.astype(BF)
        onto[b] = ones_where(iota((pins, NETS), 1) == cols[:, 1:2])
        inv[b] = jnp.broadcast_to(1.0 / jnp.maximum(jnp.sum(hit, axis=1, keepdims=True), 1.0), (NETS, F))
        pin[0, b] = dot(gath[b, :, 0:cells], x_ref[...], 1, 0).astype(BF)
        pin[1, b] = dot(gath[b, :, 0:cells], g_ref[...], 1, 0).astype(BF)

    lists(0, ref_ref[0:1, :], net_ref[0:1, :])
    grads[...] = jnp.zeros_like(grads)
    bsum[...] = jnp.zeros_like(bsum)
    arrived(ids_recv.at[pl.ds(0, 3)], 1)
    ids = ids_recv[0] + ids_recv[1] + ids_recv[2] + ids_recv[3]
    lists(1, ids[0:1, :], ids[1:2, :])
    idx_row = jnp.broadcast_to(idx_col.astype(F32), (outer, 8)).T[0:1, :].astype(I32)
    sel_t[...] = ones_where(iota((cells, outer), 0) == idx_row)
    for load in loads:
        load.wait()

    most = pl.ds(0, (nc - 1) * slots)
    arrived(halo.at[core, most], 0)
    send(halo.at[core], halo.at[core], 2, near)

    def fetch(k):
        for b in range(2):
            pin[k, b] += dot(gath[b, :, cells:], halo[k], 1, 0).astype(BF)

    fetch(core)
    arrived(halo.at[core], 2)
    fetch(other)

    for b in range(2):
        px = pin[0, b]
        pin_xt[b] = px.astype(F32).T.astype(BF)
        nf = (dot(into[b], px, 1, 0) * inv[b]).astype(BF)
        net_feat[b] = nf
        net_feat_t[b] = nf.astype(F32).T.astype(BF)

    def item(b, hb, slot):
        cols = rows_at(hb, HB)
        place = rows_at(slot, HB)
        w_in = w_in_ref[:, cols]
        w_net = w_net_ref[:, cols]
        w_out = w_out_ref[cols, :]
        px = pin[0, b]
        pg = pin[1, b]
        net_pre = dot(net_feat[b], w_net, 1, 0).astype(BF)
        pre_act = dot(px, w_in, 1, 0) + dot(onto[b], net_pre, 1, 0) + bias_ref[:, cols]
        act, slope = gelu_pair(pre_act)
        hidden = act.astype(BF)
        hid[:, place] = hidden
        pre_grad = (dot(pg, w_out, 1, 1) * slope).astype(BF)
        net_grad = dot(into[b], pre_grad, 1, 0).astype(BF)
        slope_g[:, place] = pre_grad
        net_g[:, place] = net_grad
        terms = (
            dot(pin_xt[b], pre_grad, 1, 0),
            dot(hidden, pg, 0, 0),
            dot(net_feat_t[b], net_grad, 1, 0),
        )
        for h in range(2):
            for t in range(3):
                grads[h, hb * 3 + t] += terms[t][:, h * 128 : h * 128 + 128]
        bias_row = jnp.sum(pre_grad.astype(F32), axis=0, keepdims=True)
        for h in range(2):
            bsum[h] += jnp.where(iota((16, 128), 0) == hb, bias_row[:, h * 128 : h * 128 + 128], 0.0)

    g_rows = rows_at(p, gr)

    def spread_grads(hb):
        part = pl.ds(hb * 3, 3)
        arrived(grad_in.at[part], 3 + hb)
        g_send[part] = (grads[core, part] + grad_in[part]).astype(BF)

        pair = pl.ds(hb * 3, 2)

        def push_xy(k, _):
            t = lax.rem(p + k, peers)
            send(g_send.at[pair, rows_at(t, gr), :], g_recv.at[hb, p], 7 + hb, xy_dev(t))
            return 0

        def push_q(k, _):
            t = lax.rem(z + k, zs)
            send(g_send.at[hb * 3 + 2, rows_at(t, zq), :], q_recv.at[hb, z], 25 + hb, z_dev(t))
            return 0

        lax.fori_loop(1, peers, push_xy, 0)
        lax.fori_loop(1, zs, push_q, 0)
        g_recv[hb, p] = g_send[pair, g_rows, :]
        q_recv[hb, z] = g_send[hb * 3 + 2, rows_at(z, zq), :]

    item(1, n, 4)

    def turn(hb, _):
        item(0, hb, hb)
        part = pl.ds(hb * 3, 3)
        send(grads.at[other, part], grad_in.at[part], 3 + hb, near)

        @pl.when(hb > 0)
        def _():
            spread_grads(hb - 1)

        return 0

    lax.fori_loop(0, 4, turn, 0)
    send(bsum.at[other], b_in, 11, near)
    wide = 4 * HB
    extra = rows_at(n, HB)
    pairs = (
        (slice(0, wide), w_in_ref[...], w_net_ref[...], w_out_ref[...]),
        (slice(wide, wide + HB), w_in_ref[:, extra], w_net_ref[:, extra], w_out_ref[extra, :]),
    )
    backs = []
    for b, (cols, w_in, w_net, w_out) in enumerate(pairs):
        mine_b = slice(b * pins, (b + 1) * pins)
        vals[0, mine_b, :] = dot(hid[:, cols], w_out, 1, 0).astype(BF)
        feat_grad = (dot(net_g[:, cols], w_net, 1, 1) * inv[b]).astype(BF)
        vals[1, mine_b, :] = (dot(slope_g[:, cols], w_in, 1, 1) + dot(onto[b], feat_grad, 1, 0)).astype(BF)
    spread_grads(3)

    def scatter(k):
        far_buf[k] = dot(scat[cells:, :], vals[k], 1, 0)
        near_buf[k] = dot(scat[0:cells, :], vals[k], 1, 0)

    def over_z(buf, dst, i):
        def push_z(k, _):
            send(buf, dst.at[z], i, z_dev(lax.rem(z + k, zs)))
            return 0

        lax.fori_loop(1, zs, push_z, 0)
        dst[z] = buf[...]

    def reduce_z(hb):
        arrived(g_recv.at[hb, pl.ds(0, peers - 1)], 7 + hb)
        total = g_recv[hb, 0].astype(F32)
        for k in range(1, peers):
            total += g_recv[hb, k].astype(F32)
        z_send[hb] = total.reshape(2 * gr, 128).astype(BF)
        over_z(z_send.at[hb], z_recv.at[hb], 33 + hb)

    reduce_z(0)
    scatter(other)
    send(far_buf.at[other], far_in, 12, near)
    send(near_buf.at[other], near_in, 13, near)
    arrived(b_in, 11)
    b_send[...] = (bsum[core] + b_in[...]).astype(BF)

    def push_b(k, _):
        t = lax.rem(p + k, peers)
        send(b_send, b_recv.at[p], 14, xy_dev(t))
        return 0

    lax.fori_loop(1, peers, push_b, 0)
    b_recv[p] = b_send[...]
    reduce_z(1)
    scatter(core)
    reduce_z(2)

    arrived(far_in, 12)
    a2a_buf[...] = (far_buf[core] + far_in[...]).astype(BF)

    def push_back(k, _):
        d = lax.rem(c + k, nc)
        send(a2a_buf.at[rows_at(d, slots)], a2a_in.at[mine], 15, (d, n))
        return 0

    first = 1 + (nc - 1) * WAVE // 8
    lax.fori_loop(1, first, push_back, 0)
    a2a_in[mine, :] = a2a_buf[mine, :]
    arrived(near_in, 13)
    half_buf[...] = near_buf[core] + near_in[...]
    reduce_z(3)
    lax.fori_loop(first, nc, push_back, 0)

    arrived(b_recv.at[pl.ds(0, peers - 1)], 14)
    b_sum = b_recv[0].astype(F32)
    for k in range(1, peers):
        b_sum += b_recv[k].astype(F32)
    bz_send[...] = b_sum[0:8, :]
    over_z(bz_send, bz_recv, 16)

    q_sums = []
    for hb in range(4):
        arrived(q_recv.at[hb, pl.ds(0, zs - 1)], 25 + hb)
        total = q_recv[hb, 0].astype(F32)
        for k in range(1, zs):
            total += q_recv[hb, k].astype(F32)
        q_sums.append(total)
    r_send[...] = jnp.concatenate(q_sums, axis=0).reshape(peers, zz, 128)

    def push_r(k, _):
        t = lax.rem(p + k, peers)
        send(r_send.at[t], r_recv.at[p], 29, xy_dev(t))
        return 0

    lax.fori_loop(1, peers, push_r, 0)
    r_recv[p] = r_send[p]
    arrived(r_recv.at[pl.ds(0, peers - 1)], 29)
    rsum = r_recv[0]
    for k in range(1, peers):
        rsum += r_recv[k]
    r_fin[...] = rsum

    def push_ra(k, _):
        send(r_fin, r_all.at[p], 17, xy_dev(lax.rem(p + k, peers)))
        return 0

    lax.fori_loop(1, peers, push_ra, 0)
    r_all[p] = rsum

    xn = peers // 4
    x_at = p // 4
    y_at = lax.rem(p, 4)
    one, two = pl.ds(0, 4), pl.ds(4, 4)

    def to_x(k):
        return xy_dev(lax.rem(x_at + k, xn) * 4 + y_at)

    def to_y(k):
        return xy_dev(x_at * 4 + lax.rem(y_at + k, 4))

    for hb in range(4):
        arrived(z_recv.at[hb, pl.ds(0, zs - 1)], 33 + hb)
        total = z_recv[hb, 0].astype(F32)
        for k in range(1, zs):
            total += z_recv[hb, k].astype(F32)
        g_fin[2 * hb : 2 * hb + 2] = total.astype(BF).reshape(2, gr, 128)
    for k in range(1, xn):
        send(g_fin.at[one], gout_ref.at[core, one, x_at, y_at], 20, to_x(k))
    for k in range(1, 4):
        send(g_fin.at[two], gout_ref.at[core, two, x_at, y_at], 22, to_y(k))
    gout_ref[core, :, x_at, y_at] = g_fin[...]

    arrived(r_all.at[pl.ds(0, peers - 1)], 17)
    gz_fin[...] = r_all[...].reshape(4, zq, 128).astype(BF)
    z_rows = rows_at(z, zq)

    def push_gz(k, _):
        send(gz_fin, gz_ref.at[core, :, z_rows, :], 30, z_dev(lax.rem(z + k, zs)))
        return 0

    lax.fori_loop(1, zs, push_gz, 0)
    gz_ref[core, :, z_rows, :] = gz_fin[...]

    if xn > 1:
        arrived(gout_ref.at[core, one, pl.ds(0, xn - 1), 0], 20)
    for k in range(1, 4):
        send(gout_ref.at[core, one, :, y_at], gout_ref.at[core, one, :, y_at], 21, to_y(k))
    arrived(gout_ref.at[core, two, 0, pl.ds(0, 3)], 22)
    for k in range(1, xn):
        send(gout_ref.at[core, two, x_at], gout_ref.at[core, two, x_at], 23, to_x(k))

    arrived(bz_recv.at[pl.ds(0, zs - 1)], 16)
    b_all = bz_recv[0]
    for k in range(1, zs):
        b_all += bz_recv[k]
    bout_ref[core] = b_all
    send(bout_ref.at[core], bout_ref.at[core], 18, near)

    arrived(a2a_in.at[most], 15)
    half_buf[...] += dot(sel_t[...], a2a_in[...], 1, 0)
    fin[...] = half_buf[...].astype(BF)
    qr = cells // 4
    ours = rows_at(n, qr)
    for k, q in enumerate((mate, across, 3 - n)):
        send(fin.at[rows_at(q, qr)], half_in.at[k], 19, (c, q))

    arrived(gout_ref.at[core, one, :, pl.ds(0, 3)], 21)
    if xn > 1:
        arrived(gout_ref.at[core, two, pl.ds(0, xn - 1)], 23)
    send(gout_ref.at[core], gout_ref.at[core], 24, near)

    zmost = gz_ref.at[core, :, pl.ds(0, (zs - 1) * zq), :]
    arrived(zmost, 30)
    send(gz_ref.at[core], gz_ref.at[core], 32, near)

    arrived(half_in, 19)
    kept = half_buf[ours, :] + half_in[1].astype(F32)
    swapped = half_in[0].astype(F32) + half_in[2].astype(F32)
    as_x = jnp.where(core == 0, kept, swapped)
    as_g = jnp.where(core == 0, swapped, kept)
    out_ref[0] = (as_x + x_ref[ours, :].astype(F32)).astype(BF)
    out_ref[1] = (as_g + g_ref[ours, :].astype(F32)).astype(BF)
    arrived(bout_ref.at[core], 18)

    left(halo.at[core, most], 0)
    left(ids_recv.at[pl.ds(0, 3)], 1)
    left(halo.at[core], 2)
    for hb in range(4):
        left(grad_in.at[pl.ds(hb * 3, 3)], 3 + hb)
        left(g_recv.at[hb, pl.ds(0, peers - 1)], 7 + hb)
        left(q_recv.at[hb, pl.ds(0, zs - 1)], 25 + hb)
        left(z_recv.at[hb, pl.ds(0, zs - 1)], 33 + hb)
    left(b_in, 11)
    left(far_in, 12)
    left(near_in, 13)
    left(b_recv.at[pl.ds(0, peers - 1)], 14)
    left(a2a_in.at[most], 15)
    left(bz_recv.at[pl.ds(0, zs - 1)], 16)
    left(r_all.at[pl.ds(0, peers - 1)], 17)
    left(bout_ref.at[core], 18)
    left(r_recv.at[pl.ds(0, peers - 1)], 29)
    left(zmost, 30)
    left(half_in, 19)
    left(gout_ref.at[core, one, :, pl.ds(0, 3)], 21)
    left(gout_ref.at[core, two, 0, pl.ds(0, 3)], 22)
    if xn > 1:
        left(gout_ref.at[core, one, pl.ds(0, xn - 1), 0], 20)
        left(gout_ref.at[core, two, pl.ds(0, xn - 1)], 23)
    arrived(gout_ref.at[core], 24)
    left(gout_ref.at[core], 24)
    arrived(gz_ref.at[core], 32)
    left(gz_ref.at[core], 32)


def finish_kernel(outs_ref, gout_ref, gz_ref, bout_ref, y_ref, x_ref, gin_ref, gnet_ref, gbias_ref, gout_full,
                  gin, gnet, gfull, gbias, sem):
    copies = []

    def put(src, dst):
        copies.append(pltpu.make_async_copy(src, dst, sem.at[len(copies)]))
        copies[-1].start()

    put(outs_ref.at[0], y_ref)
    put(outs_ref.at[1], x_ref)
    for hb in range(4):
        block = slice(hb * 256, hb * 256 + 256)
        for h in range(2):
            cols = slice(hb * 256 + h * 128, hb * 256 + h * 128 + 128)
            gin[:, cols] = gout_ref[h, hb * 2].astype(F32)
            gfull[block, h * 128 : h * 128 + 128] = gout_ref[h, hb * 2 + 1].astype(F32)
            gnet[:, cols] = gz_ref[h, hb].astype(F32)
            gbias[:, cols] = bout_ref[h, hb : hb + 1, :]
        put(gin.at[:, block], gin_ref.at[:, block])
        put(gnet.at[:, block], gnet_ref.at[:, block])
        put(gfull.at[block], gout_full.at[block])
    put(gbias, gbias_ref)
    for copy in copies:
        copy.wait()


def shape(dims, kind):
    return jax.ShapeDtypeStruct(dims, kind)


def local(nc, zs, cell_feat, out_grad, w_in, w_net, bias, w_out, send_idx, pin_net, pin_ref, block_count):
    rows = cell_feat.shape[0]
    slots = send_idx.shape[2]
    outer = nc * slots
    pins = pin_ref.shape[3]
    hidden = w_in.shape[1]
    peers = 2 * nc // zs
    gr = 256 // peers
    zq = 256 // zs
    zz = 4 * zq // peers
    dma = pltpu.SemaphoreType.DMA
    vm = pltpu.VMEM

    outs, gout, gz, bout = pl.pallas_call(
        functools.partial(layer_kernel, nc, zs, slots),
        out_shape=(shape((2, rows // 4, F), BF), shape((2, 8, peers // 4, 4, gr, 128), BF),
                   shape((2, 4, 256, 128), BF), shape((2, 8, 128), F32)),
        in_specs=[VM] * 6 + [HBM, HBM, VM, HBM],
        out_specs=(VM,) * 4,
        scratch_shapes=[
            vm((F, hidden), BF),
            vm((F, hidden), BF),
            vm((hidden, F), BF),
            vm((outer, F), BF),
            vm((2, outer, F), BF),
            vm((8, pins), I32),
            vm((4, 8, pins), I32),
            vm((rows, outer), BF),
            vm((2, pins, rows + outer), BF),
            vm((rows + outer, 2 * pins), BF),
            vm((2, 2, pins, F), BF),
            vm((2, F, pins), BF),
            vm((2, NETS, pins), BF),
            vm((2, pins, NETS), BF),
            vm((2, NETS, F), BF),
            vm((2, F, NETS), BF),
            vm((2, NETS, F), F32),
            vm((pins, 5 * HB), BF),
            vm((pins, 5 * HB), BF),
            vm((NETS, 5 * HB), BF),
            vm((2, 2 * pins, F), BF),
            vm((2, 16, 128), F32),
            vm((2, 12, 256, 128), F32),
            vm((12, 256, 128), F32),
            vm((12, 256, 128), BF),
            vm((4, peers, 2, gr, 128), BF),
            vm((16, 128), F32),
            vm((16, 128), BF),
            vm((peers, 16, 128), BF),
            vm((2, outer, F), F32),
            vm((outer, F), F32),
            vm((2, rows, F), F32),
            vm((rows, F), F32),
            vm((outer, F), BF),
            vm((outer, F), BF),
            vm((rows, F), F32),
            vm((3, rows // 4, F), BF),
            vm((rows, F), BF),
            vm((4, 2 * gr, 128), BF),
            vm((4, zs, 2 * gr, 128), BF),
            vm((8, 128), F32),
            vm((zs, 8, 128), F32),
            vm((8, gr, 128), BF),
            vm((4, zs, zq, 128), BF),
            vm((peers, zz, 128), F32),
            vm((peers, zz, 128), F32),
            vm((zz, 128), F32),
            vm((peers, zz, 128), F32),
            vm((4, zq, 128), BF),
            dma((3,)),
            dma((37,)),
            dma((37,)),
        ],
        compiler_params=pltpu.CompilerParams(collective_id=0, has_side_effects=True, vmem_limit_bytes=48 << 20),
        name="layer",
    )(*[
        pltpu.with_memory_space_constraint(v, pltpu.HBM)
        for v in (cell_feat, out_grad, send_idx[0].T, pin_net.reshape(2, pins), pin_ref.reshape(2, pins))
    ], block_count, *[
        pltpu.with_memory_space_constraint(v, pltpu.HBM) for v in (w_in, w_net, bias.reshape(1, hidden), w_out)
    ])

    updated, cell_grad, grad_in, grad_net, grad_bias, grad_out = pl.pallas_call(
        finish_kernel,
        out_shape=(
            shape((rows // 4, F), BF), shape((rows // 4, F), BF), shape((F, hidden), F32),
            shape((F, hidden), F32), shape((1, hidden), F32), shape((hidden, F), F32),
        ),
        in_specs=[VM] * 4,
        out_specs=(ANY,) * 6,
        scratch_shapes=[
            vm((F, hidden), F32), vm((F, hidden), F32), vm((hidden, F), F32), vm((1, hidden), F32), dma((15,)),
        ],
        compiler_params=pltpu.CompilerParams(vmem_limit_bytes=12 << 20),
        name="finish",
    )(outs, gout.reshape(2, 8, 256, 128), gz, bout)
    return (updated, cell_grad, grad_in, grad_net, grad_bias.reshape(hidden), grad_out)


def solution(mesh):
    nc = mesh.shape["cell"]
    placed = (
        P("cell", None), P("cell", None), P(), P(), P(), P(),
        P("cell", None, None), P("cell", "net", None, None), P("cell", "net", None, None), P("cell", "net"),
    )
    return jax.shard_map(
        functools.partial(local, nc, Z_SIZE),
        mesh=mesh,
        in_specs=placed,
        out_specs=(P(("cell", "net"), None), P(("cell", "net"), None), P(), P(), P(), P()),
        check_vma=False,
    )
```

```python
import functools

import jax
import jax.numpy as jnp
from jax import lax
from jax.experimental import pallas as pl
from jax.experimental.pallas import tpu as pltpu
from jax.sharding import PartitionSpec as P

MESH = pl.DeviceIdType.MESH
NETS = 128
F = 256
HB = 256
VM = pl.BlockSpec(memory_space=pltpu.VMEM)
ANY = pl.BlockSpec(memory_space=pl.ANY)
HBM = pl.BlockSpec(memory_space=pltpu.HBM)
BF = jnp.bfloat16
F32 = jnp.float32
I32 = jnp.int32
Z_SIZE = 8
WAVE = 2


def dot(a, b, ca, cb):
    return lax.dot_general(a, b, (((ca,), (cb,)), ((), ())), preferred_element_type=F32)


def remote(src, dst, sems, dev):
    return pltpu.make_async_remote_copy(
        src_ref=src, dst_ref=dst, send_sem=sems[0], recv_sem=sems[1], device_id=dev, device_id_type=MESH
    )


def iota(dims, axis):
    return lax.broadcasted_iota(I32, dims, axis)


def ones_where(mask):
    return mask.astype(F32).astype(BF)


def gelu_pair(x):
    k = 0.7978845608028654
    q = k * 0.044715
    sq = x * x
    half = 0.5 + 0.5 * jnp.tanh(x * (k + q * sq))
    act = x * half
    return act, half + (act - act * half) * (2.0 * k + 6.0 * q * sq)


def layer_kernel(nc, zs, slots,
                 x_hbm, g_hbm, idx_hbm, net_hbm, ref_hbm, cnt_ref, w_in_hbm, w_net_hbm, bias_hbm, w_out_hbm,
                 out_ref, gout_ref, gz_ref, bout_ref,
                 x_ref, g_ref, idx_ref, net_ref, ref_ref, bias_ref, w_in_ref, w_net_ref, w_out_ref, send_buf, halo, ids_buf, ids_recv, sel_t, gath, scat, pin, pin_xt,
                 into, onto, net_feat, net_feat_t, inv, hid, slope_g, net_g, vals, bsum, grads, grad_in, g_send, g_recv,
                 b_in, b_send, b_recv, far_buf, far_in, near_buf, near_in, a2a_buf, a2a_in, half_buf, half_in, fin,
                 z_send, z_recv, bz_send, bz_recv, g_fin, q_recv, r_send, r_recv, r_fin, r_all, gz_fin, w_sem, send_sem, recv_sem):
    c = lax.axis_index("cell")
    n = lax.axis_index("net")
    core = lax.rem(n, 2)
    other = 1 - core
    y_hi = n // 2
    mate = n + 1 - 2 * core
    across = lax.rem(n + 2, 4)
    xy = nc // zs
    peers = 2 * xy
    gr = 256 // peers
    zq = 256 // zs
    zz = 4 * zq // peers
    z = c // xy
    base = z * xy
    p = lax.rem(c, xy) * 2 + y_hi
    near = (c, mate)
    cells = x_ref.shape[0]
    outer = nc * slots
    pins = ref_ref.shape[1]
    loads = [
        pltpu.make_async_copy(src, dst, w_sem.at[i])
        for i, (src, dst) in enumerate((
            (idx_hbm, idx_ref), (x_hbm, x_ref), (g_hbm, g_ref), (net_hbm, net_ref), (ref_hbm, ref_ref),
            (bias_hbm, bias_ref), (w_in_hbm, w_in_ref), (w_net_hbm, w_net_ref), (w_out_hbm, w_out_ref),
        ))
    ]
    for load in loads:
        load.start()
    sem = lambda i: (send_sem.at[i], recv_sem.at[i])

    def send(src, dst, i, dev):
        remote(src, dst, sem(i), dev).start()

    def arrived(ref, i):
        remote(ref, ref, sem(i), near).wait_recv()

    def left(ref, i):
        remote(ref, ref, sem(i), near).wait_send()

    def xy_dev(t):
        return (base + t // 2, lax.rem(t, 2) * 2 + core)

    def z_dev(t):
        return (t * xy + lax.rem(c, xy), n)

    def rows_at(k, size):
        return pl.ds(pl.multiple_of(k * size, size), size)

    barrier = pltpu.get_barrier_semaphore()

    def hail(dev):
        pl.semaphore_signal(barrier, inc=1, device_id=dev, device_id_type=MESH)

    def greet(k, _):
        hail((lax.rem(c + k, nc), n))
        return 0

    def greet_across(k, _):
        hail((base + k, across))
        return 0

    lax.fori_loop(1, nc, greet, 0)
    lax.fori_loop(0, xy, greet_across, 0)
    hail(near)
    hail((c, 3 - n))

    for load in loads[:5]:
        load.wait()
    idx = idx_ref[...]
    high = (idx // 2).astype(F32).astype(BF)
    low = lax.rem(idx, 2).astype(F32).astype(BF)
    pick = ones_where(iota((outer, nc), 0) // slots == iota((outer, nc), 1))
    spread = 2.0 * dot(pick, high, 1, 1) + dot(pick, low, 1, 1)
    keep = lax.rem(iota((outer, slots), 0), slots) == iota((outer, slots), 1)
    idx_col = jnp.sum(jnp.where(keep, spread, 0.0), axis=1, keepdims=True).astype(I32)
    table = jnp.where(core == 0, x_ref[...].astype(F32), g_ref[...].astype(F32)).astype(BF)
    send_buf[...] = dot(ones_where(iota((outer, cells), 1) == idx_col), table, 1, 0).astype(BF)
    live = (cnt_ref[...] == 2).astype(I32)
    ids_buf[...] = jnp.zeros_like(ids_buf)
    ids_buf[0:1, :] = ref_ref[1:2, :] * live
    ids_buf[1:2, :] = net_ref[1:2, :] * live

    pl.semaphore_wait(barrier, nc - 1 + xy + 2)

    mine = rows_at(c, slots)

    lanes, relay_lanes = pl.ds(0, 128), pl.ds(128, 128)
    relays = lax.rem(z, 2) == y_hi

    @pl.when(relays)
    def _():
        def push_relay(k, _):
            d = lax.rem(c + k, nc)
            send(send_buf.at[rows_at(d, slots), relay_lanes], halo.at[core, mine, relay_lanes], 37, (d, n))
            return 0

        lax.fori_loop(1, nc, push_relay, 0)

    def push(k, _):
        d = lax.rem(c + k, nc)
        send(send_buf.at[rows_at(d, slots), lanes], halo.at[core, mine, lanes], 0, (d, n))
        return 0

    lax.fori_loop(1, nc, push, 0)
    for m in range(1, 4):
        send(ids_buf, ids_recv.at[n], 1, (c, lax.rem(n + m, 4)))
    halo[core, mine, 0:128] = send_buf[mine, 0:128]

    @pl.when(relays)
    def _():
        halo[core, mine, 128:256] = send_buf[mine, 128:256]

    ids_recv[n] = ids_buf[...]

    def lists(b, refs, nets):
        ids = jnp.concatenate([refs, nets, jnp.zeros((6, pins), I32)], axis=0).astype(F32)
        cols = ids.T.astype(I32)
        gath[b] = ones_where(iota((pins, cells + outer), 1) == cols[:, 0:1])
        scat[:, b * pins : (b + 1) * pins] = ones_where(iota((cells + outer, pins), 0) == refs)
        hit = (iota((NETS, pins), 0) == nets).astype(F32)
        into[b] = hit.astype(BF)
        onto[b] = ones_where(iota((pins, NETS), 1) == cols[:, 1:2])
        inv[b] = jnp.broadcast_to(1.0 / jnp.maximum(jnp.sum(hit, axis=1, keepdims=True), 1.0), (NETS, F))
        pin[0, b] = dot(gath[b, :, 0:cells], x_ref[...], 1, 0).astype(BF)
        pin[1, b] = dot(gath[b, :, 0:cells], g_ref[...], 1, 0).astype(BF)

    lists(0, ref_ref[0:1, :], net_ref[0:1, :])
    grads[...] = jnp.zeros_like(grads)
    bsum[...] = jnp.zeros_like(bsum)
    arrived(ids_recv.at[pl.ds(0, 3)], 1)
    ids = ids_recv[0] + ids_recv[1] + ids_recv[2] + ids_recv[3]
    some = outer // 2

    @pl.when(relays)
    def _():
        arrived(halo.at[core, pl.ds(0, some - slots), relay_lanes], 37)

    @pl.when(jnp.logical_not(relays))
    def _():
        arrived(halo.at[core, pl.ds(0, some), relay_lanes], 37)

    for k in range(zs // 2):
        plane = halo.at[core, rows_at(y_hi + 2 * k, xy * slots), relay_lanes]
        send(plane, plane, 38, (c, across))
    lists(1, ids[0:1, :], ids[1:2, :])
    idx_row = jnp.broadcast_to(idx_col.astype(F32), (outer, 8)).T[0:1, :].astype(I32)
    sel_t[...] = ones_where(iota((cells, outer), 0) == idx_row)
    for load in loads[5:]:
        load.wait()

    most = pl.ds(0, (nc - 1) * slots)
    arrived(halo.at[core, most, lanes], 0)
    arrived(halo.at[core, pl.ds(0, some), relay_lanes], 38)
    send(halo.at[core], halo.at[core], 2, near)

    def fetch(k):
        for b in range(2):
            pin[k, b] += dot(gath[b, :, cells:], halo[k], 1, 0).astype(BF)

    fetch(core)
    arrived(halo.at[core], 2)
    fetch(other)

    for b in range(2):
        px = pin[0, b]
        pin_xt[b] = px.astype(F32).T.astype(BF)
        nf = (dot(into[b], px, 1, 0) * inv[b]).astype(BF)
        net_feat[b] = nf
        net_feat_t[b] = nf.astype(F32).T.astype(BF)

    def item(b, hb, slot):
        cols = rows_at(hb, HB)
        place = rows_at(slot, HB)
        w_in = w_in_ref[:, cols]
        w_net = w_net_ref[:, cols]
        w_out = w_out_ref[cols, :]
        px = pin[0, b]
        pg = pin[1, b]
        net_pre = dot(net_feat[b], w_net, 1, 0).astype(BF)
        pre_act = dot(px, w_in, 1, 0) + dot(onto[b], net_pre, 1, 0) + bias_ref[:, cols]
        act, slope = gelu_pair(pre_act)
        hidden = act.astype(BF)
        hid[:, place] = hidden
        pre_grad = (dot(pg, w_out, 1, 1) * slope).astype(BF)
        net_grad = dot(into[b], pre_grad, 1, 0).astype(BF)
        slope_g[:, place] = pre_grad
        net_g[:, place] = net_grad
        terms = (
            dot(pin_xt[b], pre_grad, 1, 0),
            dot(hidden, pg, 0, 0),
            dot(net_feat_t[b], net_grad, 1, 0),
        )
        for h in range(2):
            for t in range(3):
                grads[h, hb * 3 + t] += terms[t][:, h * 128 : h * 128 + 128]
        bias_row = jnp.sum(pre_grad.astype(F32), axis=0, keepdims=True)
        for h in range(2):
            bsum[h] += jnp.where(iota((16, 128), 0) == hb, bias_row[:, h * 128 : h * 128 + 128], 0.0)

    g_rows = rows_at(p, gr)

    def spread_grads(hb):
        part = pl.ds(hb * 3, 3)
        arrived(grad_in.at[part], 3 + hb)
        g_send[part] = (grads[core, part] + grad_in[part]).astype(BF)

        pair = pl.ds(hb * 3, 2)

        def push_xy(k, _):
            t = lax.rem(p + k, peers)
            send(g_send.at[pair, rows_at(t, gr), :], g_recv.at[hb, p], 7 + hb, xy_dev(t))
            return 0

        def push_q(k, _):
            t = lax.rem(z + k, zs)
            send(g_send.at[hb * 3 + 2, rows_at(t, zq), :], q_recv.at[hb, z], 25 + hb, z_dev(t))
            return 0

        lax.fori_loop(1, peers, push_xy, 0)
        lax.fori_loop(1, zs, push_q, 0)
        g_recv[hb, p] = g_send[pair, g_rows, :]
        q_recv[hb, z] = g_send[hb * 3 + 2, rows_at(z, zq), :]

    item(1, n, 4)

    def turn(hb, _):
        item(0, hb, hb)
        part = pl.ds(hb * 3, 3)
        send(grads.at[other, part], grad_in.at[part], 3 + hb, near)

        @pl.when(hb > 0)
        def _():
            spread_grads(hb - 1)

        return 0

    lax.fori_loop(0, 4, turn, 0)
    send(bsum.at[other], b_in, 11, near)
    wide = 4 * HB
    extra = rows_at(n, HB)
    pairs = (
        (slice(0, wide), w_in_ref[...], w_net_ref[...], w_out_ref[...]),
        (slice(wide, wide + HB), w_in_ref[:, extra], w_net_ref[:, extra], w_out_ref[extra, :]),
    )
    backs = []
    for b, (cols, w_in, w_net, w_out) in enumerate(pairs):
        mine_b = slice(b * pins, (b + 1) * pins)
        vals[0, mine_b, :] = dot(hid[:, cols], w_out, 1, 0).astype(BF)
        feat_grad = (dot(net_g[:, cols], w_net, 1, 1) * inv[b]).astype(BF)
        vals[1, mine_b, :] = (dot(slope_g[:, cols], w_in, 1, 1) + dot(onto[b], feat_grad, 1, 0)).astype(BF)
    spread_grads(3)

    def scatter(k):
        far_buf[k] = dot(scat[cells:, :], vals[k], 1, 0)
        near_buf[k] = dot(scat[0:cells, :], vals[k], 1, 0)

    def over_z(buf, dst, i):
        def push_z(k, _):
            send(buf, dst.at[z], i, z_dev(lax.rem(z + k, zs)))
            return 0

        lax.fori_loop(1, zs, push_z, 0)
        dst[z] = buf[...]

    def reduce_z(hb):
        arrived(g_recv.at[hb, pl.ds(0, peers - 1)], 7 + hb)
        total = g_recv[hb, 0].astype(F32)
        for k in range(1, peers):
            total += g_recv[hb, k].astype(F32)
        z_send[hb] = total.reshape(2 * gr, 128).astype(BF)
        over_z(z_send.at[hb], z_recv.at[hb], 33 + hb)

    reduce_z(0)
    scatter(other)
    send(far_buf.at[other], far_in, 12, near)
    send(near_buf.at[other], near_in, 13, near)
    arrived(b_in, 11)
    b_send[...] = (bsum[core] + b_in[...]).astype(BF)

    def push_b(k, _):
        t = lax.rem(p + k, peers)
        send(b_send, b_recv.at[p], 14, xy_dev(t))
        return 0

    lax.fori_loop(1, peers, push_b, 0)
    b_recv[p] = b_send[...]
    reduce_z(1)
    scatter(core)
    reduce_z(2)

    arrived(far_in, 12)
    a2a_buf[...] = (far_buf[core] + far_in[...]).astype(BF)

    def push_back(k, _):
        d = lax.rem(c + k, nc)
        send(a2a_buf.at[rows_at(d, slots)], a2a_in.at[mine], 15, (d, n))
        return 0

    first = 1 + (nc - 1) * WAVE // 8
    lax.fori_loop(1, first, push_back, 0)
    a2a_in[mine, :] = a2a_buf[mine, :]
    arrived(near_in, 13)
    half_buf[...] = near_buf[core] + near_in[...]
    reduce_z(3)
    lax.fori_loop(first, nc, push_back, 0)

    arrived(b_recv.at[pl.ds(0, peers - 1)], 14)
    b_sum = b_recv[0].astype(F32)
    for k in range(1, peers):
        b_sum += b_recv[k].astype(F32)
    bz_send[...] = b_sum[0:8, :]
    over_z(bz_send, bz_recv, 16)

    q_sums = []
    for hb in range(4):
        arrived(q_recv.at[hb, pl.ds(0, zs - 1)], 25 + hb)
        total = q_recv[hb, 0].astype(F32)
        for k in range(1, zs):
            total += q_recv[hb, k].astype(F32)
        q_sums.append(total)
    r_send[...] = jnp.concatenate(q_sums, axis=0).reshape(peers, zz, 128)

    def push_r(k, _):
        t = lax.rem(p + k, peers)
        send(r_send.at[t], r_recv.at[p], 29, xy_dev(t))
        return 0

    lax.fori_loop(1, peers, push_r, 0)
    r_recv[p] = r_send[p]
    arrived(r_recv.at[pl.ds(0, peers - 1)], 29)
    rsum = r_recv[0]
    for k in range(1, peers):
        rsum += r_recv[k]
    r_fin[...] = rsum

    def push_ra(k, _):
        send(r_fin, r_all.at[p], 17, xy_dev(lax.rem(p + k, peers)))
        return 0

    lax.fori_loop(1, peers, push_ra, 0)
    r_all[p] = rsum

    xn = peers // 4
    x_at = p // 4
    y_at = lax.rem(p, 4)
    one, two = pl.ds(0, 4), pl.ds(4, 4)

    def to_x(k):
        return xy_dev(lax.rem(x_at + k, xn) * 4 + y_at)

    def to_y(k):
        return xy_dev(x_at * 4 + lax.rem(y_at + k, 4))

    for hb in range(4):
        arrived(z_recv.at[hb, pl.ds(0, zs - 1)], 33 + hb)
        total = z_recv[hb, 0].astype(F32)
        for k in range(1, zs):
            total += z_recv[hb, k].astype(F32)
        g_fin[2 * hb : 2 * hb + 2] = total.astype(BF).reshape(2, gr, 128)
    for k in range(1, xn):
        send(g_fin.at[one], gout_ref.at[core, one, x_at, y_at], 20, to_x(k))
    for k in range(1, 4):
        send(g_fin.at[two], gout_ref.at[core, two, x_at, y_at], 22, to_y(k))
    gout_ref[core, :, x_at, y_at] = g_fin[...]

    arrived(r_all.at[pl.ds(0, peers - 1)], 17)
    gz_fin[...] = r_all[...].reshape(4, zq, 128).astype(BF)
    z_rows = rows_at(z, zq)

    def push_gz(k, _):
        send(gz_fin, gz_ref.at[core, :, z_rows, :], 30, z_dev(lax.rem(z + k, zs)))
        return 0

    lax.fori_loop(1, zs, push_gz, 0)
    gz_ref[core, :, z_rows, :] = gz_fin[...]

    if xn > 1:
        arrived(gout_ref.at[core, one, pl.ds(0, xn - 1), 0], 20)
    for k in range(1, 4):
        send(gout_ref.at[core, one, :, y_at], gout_ref.at[core, one, :, y_at], 21, to_y(k))
    arrived(gout_ref.at[core, two, 0, pl.ds(0, 3)], 22)
    for k in range(1, xn):
        send(gout_ref.at[core, two, x_at], gout_ref.at[core, two, x_at], 23, to_x(k))

    arrived(bz_recv.at[pl.ds(0, zs - 1)], 16)
    b_all = bz_recv[0]
    for k in range(1, zs):
        b_all += bz_recv[k]
    bout_ref[core] = b_all
    send(bout_ref.at[core], bout_ref.at[core], 18, near)

    arrived(a2a_in.at[most], 15)
    half_buf[...] += dot(sel_t[...], a2a_in[...], 1, 0)
    fin[...] = half_buf[...].astype(BF)
    qr = cells // 4
    ours = rows_at(n, qr)
    for k, q in enumerate((mate, across, 3 - n)):
        send(fin.at[rows_at(q, qr)], half_in.at[k], 19, (c, q))

    arrived(gout_ref.at[core, one, :, pl.ds(0, 3)], 21)
    if xn > 1:
        arrived(gout_ref.at[core, two, pl.ds(0, xn - 1)], 23)
    send(gout_ref.at[core], gout_ref.at[core], 24, near)

    zmost = gz_ref.at[core, :, pl.ds(0, (zs - 1) * zq), :]
    arrived(zmost, 30)
    send(gz_ref.at[core], gz_ref.at[core], 32, near)

    arrived(half_in, 19)
    kept = half_buf[ours, :] + half_in[1].astype(F32)
    swapped = half_in[0].astype(F32) + half_in[2].astype(F32)
    as_x = jnp.where(core == 0, kept, swapped)
    as_g = jnp.where(core == 0, swapped, kept)
    out_ref[0] = (as_x + x_ref[ours, :].astype(F32)).astype(BF)
    out_ref[1] = (as_g + g_ref[ours, :].astype(F32)).astype(BF)
    arrived(bout_ref.at[core], 18)

    left(halo.at[core, most, lanes], 0)
    left(halo.at[core, pl.ds(0, some), relay_lanes], 38)

    @pl.when(relays)
    def _():
        left(halo.at[core, most, relay_lanes], 37)

    left(ids_recv.at[pl.ds(0, 3)], 1)
    left(halo.at[core], 2)
    for hb in range(4):
        left(grad_in.at[pl.ds(hb * 3, 3)], 3 + hb)
        left(g_recv.at[hb, pl.ds(0, peers - 1)], 7 + hb)
        left(q_recv.at[hb, pl.ds(0, zs - 1)], 25 + hb)
        left(z_recv.at[hb, pl.ds(0, zs - 1)], 33 + hb)
    left(b_in, 11)
    left(far_in, 12)
    left(near_in, 13)
    left(b_recv.at[pl.ds(0, peers - 1)], 14)
    left(a2a_in.at[most], 15)
    left(bz_recv.at[pl.ds(0, zs - 1)], 16)
    left(r_all.at[pl.ds(0, peers - 1)], 17)
    left(bout_ref.at[core], 18)
    left(r_recv.at[pl.ds(0, peers - 1)], 29)
    left(zmost, 30)
    left(half_in, 19)
    left(gout_ref.at[core, one, :, pl.ds(0, 3)], 21)
    left(gout_ref.at[core, two, 0, pl.ds(0, 3)], 22)
    if xn > 1:
        left(gout_ref.at[core, one, pl.ds(0, xn - 1), 0], 20)
        left(gout_ref.at[core, two, pl.ds(0, xn - 1)], 23)
    arrived(gout_ref.at[core], 24)
    left(gout_ref.at[core], 24)
    arrived(gz_ref.at[core], 32)
    left(gz_ref.at[core], 32)


def finish_kernel(outs_ref, gout_ref, gz_ref, bout_ref, y_ref, x_ref, gin_ref, gnet_ref, gbias_ref, gout_full,
                  gin, gnet, gfull, gbias, sem):
    copies = []

    def put(src, dst):
        copies.append(pltpu.make_async_copy(src, dst, sem.at[len(copies)]))
        copies[-1].start()

    put(outs_ref.at[0], y_ref)
    put(outs_ref.at[1], x_ref)
    for hb in range(4):
        block = slice(hb * 256, hb * 256 + 256)
        for h in range(2):
            cols = slice(hb * 256 + h * 128, hb * 256 + h * 128 + 128)
            gin[:, cols] = gout_ref[h, hb * 2].astype(F32)
            gfull[block, h * 128 : h * 128 + 128] = gout_ref[h, hb * 2 + 1].astype(F32)
            gnet[:, cols] = gz_ref[h, hb].astype(F32)
            gbias[:, cols] = bout_ref[h, hb : hb + 1, :]
        put(gin.at[:, block], gin_ref.at[:, block])
        put(gnet.at[:, block], gnet_ref.at[:, block])
        put(gfull.at[block], gout_full.at[block])
    put(gbias, gbias_ref)
    for copy in copies:
        copy.wait()


def shape(dims, kind):
    return jax.ShapeDtypeStruct(dims, kind)


def local(nc, zs, cell_feat, out_grad, w_in, w_net, bias, w_out, send_idx, pin_net, pin_ref, block_count):
    rows = cell_feat.shape[0]
    slots = send_idx.shape[2]
    outer = nc * slots
    pins = pin_ref.shape[3]
    hidden = w_in.shape[1]
    peers = 2 * nc // zs
    gr = 256 // peers
    zq = 256 // zs
    zz = 4 * zq // peers
    dma = pltpu.SemaphoreType.DMA
    vm = pltpu.VMEM

    outs, gout, gz, bout = pl.pallas_call(
        functools.partial(layer_kernel, nc, zs, slots),
        out_shape=(shape((2, rows // 4, F), BF), shape((2, 8, peers // 4, 4, gr, 128), BF),
                   shape((2, 4, 256, 128), BF), shape((2, 8, 128), F32)),
        in_specs=[HBM] * 5 + [VM] + [HBM] * 4,
        out_specs=(VM,) * 4,
        scratch_shapes=[
            vm((rows, F), BF),
            vm((rows, F), BF),
            vm((slots, nc), I32),
            vm((2, pins), I32),
            vm((2, pins), I32),
            vm((1, hidden), F32),
            vm((F, hidden), BF),
            vm((F, hidden), BF),
            vm((hidden, F), BF),
            vm((outer, F), BF),
            vm((2, outer, F), BF),
            vm((8, pins), I32),
            vm((4, 8, pins), I32),
            vm((rows, outer), BF),
            vm((2, pins, rows + outer), BF),
            vm((rows + outer, 2 * pins), BF),
            vm((2, 2, pins, F), BF),
            vm((2, F, pins), BF),
            vm((2, NETS, pins), BF),
            vm((2, pins, NETS), BF),
            vm((2, NETS, F), BF),
            vm((2, F, NETS), BF),
            vm((2, NETS, F), F32),
            vm((pins, 5 * HB), BF),
            vm((pins, 5 * HB), BF),
            vm((NETS, 5 * HB), BF),
            vm((2, 2 * pins, F), BF),
            vm((2, 16, 128), F32),
            vm((2, 12, 256, 128), F32),
            vm((12, 256, 128), F32),
            vm((12, 256, 128), BF),
            vm((4, peers, 2, gr, 128), BF),
            vm((16, 128), F32),
            vm((16, 128), BF),
            vm((peers, 16, 128), BF),
            vm((2, outer, F), F32),
            vm((outer, F), F32),
            vm((2, rows, F), F32),
            vm((rows, F), F32),
            vm((outer, F), BF),
            vm((outer, F), BF),
            vm((rows, F), F32),
            vm((3, rows // 4, F), BF),
            vm((rows, F), BF),
            vm((4, 2 * gr, 128), BF),
            vm((4, zs, 2 * gr, 128), BF),
            vm((8, 128), F32),
            vm((zs, 8, 128), F32),
            vm((8, gr, 128), BF),
            vm((4, zs, zq, 128), BF),
            vm((peers, zz, 128), F32),
            vm((peers, zz, 128), F32),
            vm((zz, 128), F32),
            vm((peers, zz, 128), F32),
            vm((4, zq, 128), BF),
            dma((9,)),
            dma((39,)),
            dma((39,)),
        ],
        compiler_params=pltpu.CompilerParams(collective_id=0, has_side_effects=True, vmem_limit_bytes=48 << 20),
        name="layer",
    )(*[
        pltpu.with_memory_space_constraint(v, pltpu.HBM)
        for v in (cell_feat, out_grad, send_idx[0].T, pin_net.reshape(2, pins), pin_ref.reshape(2, pins))
    ], block_count, *[
        pltpu.with_memory_space_constraint(v, pltpu.HBM) for v in (w_in, w_net, bias.reshape(1, hidden), w_out)
    ])

    updated, cell_grad, grad_in, grad_net, grad_bias, grad_out = pl.pallas_call(
        finish_kernel,
        out_shape=(
            shape((rows // 4, F), BF), shape((rows // 4, F), BF), shape((F, hidden), F32),
            shape((F, hidden), F32), shape((1, hidden), F32), shape((hidden, F), F32),
        ),
        in_specs=[VM] * 4,
        out_specs=(ANY,) * 6,
        scratch_shapes=[
            vm((F, hidden), F32), vm((F, hidden), F32), vm((hidden, F), F32), vm((1, hidden), F32), dma((15,)),
        ],
        compiler_params=pltpu.CompilerParams(vmem_limit_bytes=12 << 20),
        name="finish",
    )(outs, gout.reshape(2, 8, 256, 128), gz, bout)
    return (updated, cell_grad, grad_in, grad_net, grad_bias.reshape(hidden), grad_out)


def solution(mesh):
    nc = mesh.shape["cell"]
    placed = (
        P("cell", None), P("cell", None), P(), P(), P(), P(),
        P("cell", None, None), P("cell", "net", None, None), P("cell", "net", None, None), P("cell", "net"),
    )
    return jax.shard_map(
        functools.partial(local, nc, Z_SIZE),
        mesh=mesh,
        in_specs=placed,
        out_specs=(P(("cell", "net"), None), P(("cell", "net"), None), P(), P(), P(), P()),
        check_vma=False,
    )
```

```python
import functools

import jax
import jax.numpy as jnp
from jax import lax
from jax.experimental import pallas as pl
from jax.experimental.pallas import tpu as pltpu
from jax.sharding import PartitionSpec as P

MESH = pl.DeviceIdType.MESH
NETS = 128
F = 256
HB = 256
VM = pl.BlockSpec(memory_space=pltpu.VMEM)
ANY = pl.BlockSpec(memory_space=pl.ANY)
HBM = pl.BlockSpec(memory_space=pltpu.HBM)
BF = jnp.bfloat16
F32 = jnp.float32
I32 = jnp.int32
Z_SIZE = 8
WAVE = 1


def dot(a, b, ca, cb):
    return lax.dot_general(a, b, (((ca,), (cb,)), ((), ())), preferred_element_type=F32)


def remote(src, dst, sems, dev):
    return pltpu.make_async_remote_copy(
        src_ref=src, dst_ref=dst, send_sem=sems[0], recv_sem=sems[1], device_id=dev, device_id_type=MESH
    )


def iota(dims, axis):
    return lax.broadcasted_iota(I32, dims, axis)


def ones_where(mask):
    return mask.astype(F32).astype(BF)


def gelu_pair(x):
    k = 0.7978845608028654
    q = k * 0.044715
    sq = x * x
    half = 0.5 + 0.5 * jnp.tanh(x * (k + q * sq))
    act = x * half
    return act, half + (act - act * half) * (2.0 * k + 6.0 * q * sq)


def layer_kernel(nc, zs, slots,
                 x_hbm, g_hbm, idx_hbm, net_hbm, ref_hbm, cnt_ref, w_in_hbm, w_net_hbm, bias_hbm, w_out_hbm,
                 out_ref, gout_ref, gz_ref, bout_ref,
                 x_ref, g_ref, idx_ref, net_ref, ref_ref, bias_ref, w_in_ref, w_net_ref, w_out_ref, send_buf, halo, ids_buf, ids_recv, sel_t, gath, scat, pin, pin_xt,
                 into, onto, net_feat, net_feat_t, inv, hid, slope_g, net_g, vals, bsum, grads, grad_in, g_send, g_recv,
                 b_in, b_send, b_recv, far_buf, far_in, near_buf, near_in, a2a_buf, a2a_in, half_buf, half_in, fin,
                 z_send, z_recv, bz_send, bz_recv, g_fin, q_recv, r_send, r_recv, r_fin, r_all, gz_fin, w_sem, send_sem, recv_sem):
    c = lax.axis_index("cell")
    n = lax.axis_index("net")
    core = lax.rem(n, 2)
    other = 1 - core
    y_hi = n // 2
    mate = n + 1 - 2 * core
    across = lax.rem(n + 2, 4)
    xy = nc // zs
    peers = 2 * xy
    gr = 256 // peers
    zq = 256 // zs
    zz = 4 * zq // peers
    z = c // xy
    base = z * xy
    p = lax.rem(c, xy) * 2 + y_hi
    near = (c, mate)
    cells = x_ref.shape[0]
    outer = nc * slots
    pins = ref_ref.shape[1]
    loads = [
        pltpu.make_async_copy(src, dst, w_sem.at[i])
        for i, (src, dst) in enumerate((
            (idx_hbm, idx_ref), (x_hbm, x_ref), (g_hbm, g_ref), (net_hbm, net_ref), (ref_hbm, ref_ref),
            (bias_hbm, bias_ref), (w_in_hbm, w_in_ref), (w_net_hbm, w_net_ref), (w_out_hbm, w_out_ref),
        ))
    ]
    for load in loads:
        load.start()
    sem = lambda i: (send_sem.at[i], recv_sem.at[i])

    def send(src, dst, i, dev):
        remote(src, dst, sem(i), dev).start()

    def arrived(ref, i):
        remote(ref, ref, sem(i), near).wait_recv()

    def left(ref, i):
        remote(ref, ref, sem(i), near).wait_send()

    def xy_dev(t):
        return (base + t // 2, lax.rem(t, 2) * 2 + core)

    def z_dev(t):
        return (t * xy + lax.rem(c, xy), n)

    def rows_at(k, size):
        return pl.ds(pl.multiple_of(k * size, size), size)

    barrier = pltpu.get_barrier_semaphore()

    def hail(dev):
        pl.semaphore_signal(barrier, inc=1, device_id=dev, device_id_type=MESH)

    def greet(k, _):
        hail((lax.rem(c + k, nc), n))
        return 0

    def greet_across(k, _):
        hail((base + k, across))
        return 0

    lax.fori_loop(1, nc, greet, 0)
    lax.fori_loop(0, xy, greet_across, 0)
    hail(near)
    hail((c, 3 - n))

    for load in loads[:5]:
        load.wait()
    idx = idx_ref[...]
    high = (idx // 2).astype(F32).astype(BF)
    low = lax.rem(idx, 2).astype(F32).astype(BF)
    pick = ones_where(iota((outer, nc), 0) // slots == iota((outer, nc), 1))
    spread = 2.0 * dot(pick, high, 1, 1) + dot(pick, low, 1, 1)
    keep = lax.rem(iota((outer, slots), 0), slots) == iota((outer, slots), 1)
    idx_col = jnp.sum(jnp.where(keep, spread, 0.0), axis=1, keepdims=True).astype(I32)
    table = jnp.where(core == 0, x_ref[...].astype(F32), g_ref[...].astype(F32)).astype(BF)
    send_buf[...] = dot(ones_where(iota((outer, cells), 1) == idx_col), table, 1, 0).astype(BF)
    live = (cnt_ref[...] == 2).astype(I32)
    ids_buf[...] = jnp.zeros_like(ids_buf)
    ids_buf[0:1, :] = ref_ref[1:2, :] * live
    ids_buf[1:2, :] = net_ref[1:2, :] * live

    pl.semaphore_wait(barrier, nc - 1 + xy + 2)

    mine = rows_at(c, slots)

    lanes, relay_lanes = pl.ds(0, 128), pl.ds(128, 128)
    relays = lax.rem(z, 2) == y_hi

    @pl.when(relays)
    def _():
        def push_relay(k, _):
            d = lax.rem(c + k, nc)
            send(send_buf.at[rows_at(d, slots), relay_lanes], halo.at[core, mine, relay_lanes], 37, (d, n))
            return 0

        lax.fori_loop(1, nc, push_relay, 0)

    def push(k, _):
        d = lax.rem(c + k, nc)
        send(send_buf.at[rows_at(d, slots), lanes], halo.at[core, mine, lanes], 0, (d, n))
        return 0

    lax.fori_loop(1, nc, push, 0)
    for m in range(1, 4):
        send(ids_buf, ids_recv.at[n], 1, (c, lax.rem(n + m, 4)))
    halo[core, mine, 0:128] = send_buf[mine, 0:128]

    @pl.when(relays)
    def _():
        halo[core, mine, 128:256] = send_buf[mine, 128:256]

    ids_recv[n] = ids_buf[...]

    def lists(b, refs, nets):
        ids = jnp.concatenate([refs, nets, jnp.zeros((6, pins), I32)], axis=0).astype(F32)
        cols = ids.T.astype(I32)
        gath[b] = ones_where(iota((pins, cells + outer), 1) == cols[:, 0:1])
        scat[:, b * pins : (b + 1) * pins] = ones_where(iota((cells + outer, pins), 0) == refs)
        hit = (iota((NETS, pins), 0) == nets).astype(F32)
        into[b] = hit.astype(BF)
        onto[b] = ones_where(iota((pins, NETS), 1) == cols[:, 1:2])
        inv[b] = jnp.broadcast_to(1.0 / jnp.maximum(jnp.sum(hit, axis=1, keepdims=True), 1.0), (NETS, F))
        pin[0, b] = dot(gath[b, :, 0:cells], x_ref[...], 1, 0).astype(BF)
        pin[1, b] = dot(gath[b, :, 0:cells], g_ref[...], 1, 0).astype(BF)

    lists(0, ref_ref[0:1, :], net_ref[0:1, :])
    grads[...] = jnp.zeros_like(grads)
    bsum[...] = jnp.zeros_like(bsum)
    arrived(ids_recv.at[pl.ds(0, 3)], 1)
    ids = ids_recv[0] + ids_recv[1] + ids_recv[2] + ids_recv[3]
    some = outer // 2

    @pl.when(relays)
    def _():
        arrived(halo.at[core, pl.ds(0, some - slots), relay_lanes], 37)

    @pl.when(jnp.logical_not(relays))
    def _():
        arrived(halo.at[core, pl.ds(0, some), relay_lanes], 37)

    for k in range(zs // 2):
        plane = halo.at[core, rows_at(y_hi + 2 * k, xy * slots), relay_lanes]
        send(plane, plane, 38, (c, across))
    lists(1, ids[0:1, :], ids[1:2, :])
    idx_row = jnp.broadcast_to(idx_col.astype(F32), (outer, 8)).T[0:1, :].astype(I32)
    sel_t[...] = ones_where(iota((cells, outer), 0) == idx_row)
    for load in loads[5:]:
        load.wait()

    most = pl.ds(0, (nc - 1) * slots)
    arrived(halo.at[core, most, lanes], 0)
    send(halo.at[core, :, lanes], halo.at[core, :, lanes], 2, near)
    arrived(halo.at[core, pl.ds(0, some), relay_lanes], 38)
    send(halo.at[core, :, relay_lanes], halo.at[core, :, relay_lanes], 39, near)

    def fetch(k):
        for b in range(2):
            pin[k, b] += dot(gath[b, :, cells:], halo[k], 1, 0).astype(BF)

    fetch(core)
    arrived(halo.at[core, :, lanes], 2)
    arrived(halo.at[core, :, relay_lanes], 39)
    fetch(other)

    for b in range(2):
        px = pin[0, b]
        pin_xt[b] = px.astype(F32).T.astype(BF)
        nf = (dot(into[b], px, 1, 0) * inv[b]).astype(BF)
        net_feat[b] = nf
        net_feat_t[b] = nf.astype(F32).T.astype(BF)

    def item(b, hb, slot):
        cols = rows_at(hb, HB)
        place = rows_at(slot, HB)
        w_in = w_in_ref[:, cols]
        w_net = w_net_ref[:, cols]
        w_out = w_out_ref[cols, :]
        px = pin[0, b]
        pg = pin[1, b]
        net_pre = dot(net_feat[b], w_net, 1, 0).astype(BF)
        pre_act = dot(px, w_in, 1, 0) + dot(onto[b], net_pre, 1, 0) + bias_ref[:, cols]
        act, slope = gelu_pair(pre_act)
        hidden = act.astype(BF)
        hid[:, place] = hidden
        pre_grad = (dot(pg, w_out, 1, 1) * slope).astype(BF)
        net_grad = dot(into[b], pre_grad, 1, 0).astype(BF)
        slope_g[:, place] = pre_grad
        net_g[:, place] = net_grad
        terms = (
            dot(pin_xt[b], pre_grad, 1, 0),
            dot(hidden, pg, 0, 0),
            dot(net_feat_t[b], net_grad, 1, 0),
        )
        for h in range(2):
            for t in range(3):
                grads[h, hb * 3 + t] += terms[t][:, h * 128 : h * 128 + 128]
        bias_row = jnp.sum(pre_grad.astype(F32), axis=0, keepdims=True)
        for h in range(2):
            bsum[h] += jnp.where(iota((16, 128), 0) == hb, bias_row[:, h * 128 : h * 128 + 128], 0.0)

    g_rows = rows_at(p, gr)

    def spread_grads(hb):
        part = pl.ds(hb * 3, 3)
        arrived(grad_in.at[part], 3 + hb)
        g_send[part] = (grads[core, part] + grad_in[part]).astype(BF)

        pair = pl.ds(hb * 3, 2)

        def push_xy(k, _):
            t = lax.rem(p + k, peers)
            send(g_send.at[pair, rows_at(t, gr), :], g_recv.at[hb, p], 7 + hb, xy_dev(t))
            return 0

        def push_q(k, _):
            t = lax.rem(z + k, zs)
            send(g_send.at[hb * 3 + 2, rows_at(t, zq), :], q_recv.at[hb, z], 25 + hb, z_dev(t))
            return 0

        lax.fori_loop(1, peers, push_xy, 0)
        lax.fori_loop(1, zs, push_q, 0)
        g_recv[hb, p] = g_send[pair, g_rows, :]
        q_recv[hb, z] = g_send[hb * 3 + 2, rows_at(z, zq), :]

    item(1, n, 4)

    def turn(hb, _):
        item(0, hb, hb)
        part = pl.ds(hb * 3, 3)
        send(grads.at[other, part], grad_in.at[part], 3 + hb, near)

        @pl.when(hb > 0)
        def _():
            spread_grads(hb - 1)

        return 0

    lax.fori_loop(0, 4, turn, 0)
    send(bsum.at[other], b_in, 11, near)
    wide = 4 * HB
    extra = rows_at(n, HB)
    pairs = (
        (slice(0, wide), w_in_ref[...], w_net_ref[...], w_out_ref[...]),
        (slice(wide, wide + HB), w_in_ref[:, extra], w_net_ref[:, extra], w_out_ref[extra, :]),
    )
    backs = []
    for b, (cols, w_in, w_net, w_out) in enumerate(pairs):
        mine_b = slice(b * pins, (b + 1) * pins)
        vals[0, mine_b, :] = dot(hid[:, cols], w_out, 1, 0).astype(BF)
        feat_grad = (dot(net_g[:, cols], w_net, 1, 1) * inv[b]).astype(BF)
        vals[1, mine_b, :] = (dot(slope_g[:, cols], w_in, 1, 1) + dot(onto[b], feat_grad, 1, 0)).astype(BF)
    spread_grads(3)

    def scatter_far(k):
        far_buf[k] = dot(scat[cells:, :], vals[k], 1, 0)

    def scatter_near(k):
        near_buf[k] = dot(scat[0:cells, :], vals[k], 1, 0)

    def over_z(buf, dst, i):
        def push_z(k, _):
            send(buf, dst.at[z], i, z_dev(lax.rem(z + k, zs)))
            return 0

        lax.fori_loop(1, zs, push_z, 0)
        dst[z] = buf[...]

    def reduce_z(hb):
        arrived(g_recv.at[hb, pl.ds(0, peers - 1)], 7 + hb)
        total = g_recv[hb, 0].astype(F32)
        for k in range(1, peers):
            total += g_recv[hb, k].astype(F32)
        z_send[hb] = total.reshape(2 * gr, 128).astype(BF)
        over_z(z_send.at[hb], z_recv.at[hb], 33 + hb)

    scatter_far(other)
    send(far_buf.at[other], far_in, 12, near)
    reduce_z(0)
    scatter_near(other)
    send(near_buf.at[other], near_in, 13, near)
    arrived(b_in, 11)
    b_send[...] = (bsum[core] + b_in[...]).astype(BF)

    def push_b(k, _):
        t = lax.rem(p + k, peers)
        send(b_send, b_recv.at[p], 14, xy_dev(t))
        return 0

    lax.fori_loop(1, peers, push_b, 0)
    b_recv[p] = b_send[...]
    reduce_z(1)
    scatter_far(core)
    reduce_z(2)
    arrived(far_in, 12)
    a2a_buf[...] = (far_buf[core] + far_in[...]).astype(BF)

    def push_back(k, _):
        d = lax.rem(c + k, nc)
        send(a2a_buf.at[rows_at(d, slots)], a2a_in.at[mine], 15, (d, n))
        return 0

    first = 1 + (nc - 1) * WAVE // 8
    lax.fori_loop(1, first, push_back, 0)
    a2a_in[mine, :] = a2a_buf[mine, :]
    reduce_z(3)
    lax.fori_loop(first, nc, push_back, 0)
    scatter_near(core)
    arrived(near_in, 13)
    half_buf[...] = near_buf[core] + near_in[...]

    arrived(b_recv.at[pl.ds(0, peers - 1)], 14)
    b_sum = b_recv[0].astype(F32)
    for k in range(1, peers):
        b_sum += b_recv[k].astype(F32)
    bz_send[...] = b_sum[0:8, :]
    over_z(bz_send, bz_recv, 16)

    q_sums = []
    for hb in range(4):
        arrived(q_recv.at[hb, pl.ds(0, zs - 1)], 25 + hb)
        total = q_recv[hb, 0].astype(F32)
        for k in range(1, zs):
            total += q_recv[hb, k].astype(F32)
        q_sums.append(total)
    r_send[...] = jnp.concatenate(q_sums, axis=0).reshape(peers, zz, 128)

    def push_r(k, _):
        t = lax.rem(p + k, peers)
        send(r_send.at[t], r_recv.at[p], 29, xy_dev(t))
        return 0

    lax.fori_loop(1, peers, push_r, 0)
    r_recv[p] = r_send[p]
    arrived(r_recv.at[pl.ds(0, peers - 1)], 29)
    rsum = r_recv[0]
    for k in range(1, peers):
        rsum += r_recv[k]
    r_fin[...] = rsum

    def push_ra(k, _):
        send(r_fin, r_all.at[p], 17, xy_dev(lax.rem(p + k, peers)))
        return 0

    lax.fori_loop(1, peers, push_ra, 0)
    r_all[p] = rsum

    xn = peers // 4
    x_at = p // 4
    y_at = lax.rem(p, 4)
    one, two = pl.ds(0, 4), pl.ds(4, 4)

    def to_x(k):
        return xy_dev(lax.rem(x_at + k, xn) * 4 + y_at)

    def to_y(k):
        return xy_dev(x_at * 4 + lax.rem(y_at + k, 4))

    for hb in range(4):
        arrived(z_recv.at[hb, pl.ds(0, zs - 1)], 33 + hb)
        total = z_recv[hb, 0].astype(F32)
        for k in range(1, zs):
            total += z_recv[hb, k].astype(F32)
        g_fin[2 * hb : 2 * hb + 2] = total.astype(BF).reshape(2, gr, 128)
    for k in range(1, xn):
        send(g_fin.at[one], gout_ref.at[core, one, x_at, y_at], 20, to_x(k))
    for k in range(1, 4):
        send(g_fin.at[two], gout_ref.at[core, two, x_at, y_at], 22, to_y(k))
    gout_ref[core, :, x_at, y_at] = g_fin[...]

    arrived(r_all.at[pl.ds(0, peers - 1)], 17)
    gz_fin[...] = r_all[...].reshape(4, zq, 128).astype(BF)
    z_rows = rows_at(z, zq)

    def push_gz(k, _):
        send(gz_fin, gz_ref.at[core, :, z_rows, :], 30, z_dev(lax.rem(z + k, zs)))
        return 0

    lax.fori_loop(1, zs, push_gz, 0)
    gz_ref[core, :, z_rows, :] = gz_fin[...]

    if xn > 1:
        arrived(gout_ref.at[core, one, pl.ds(0, xn - 1), 0], 20)
    for k in range(1, 4):
        send(gout_ref.at[core, one, :, y_at], gout_ref.at[core, one, :, y_at], 21, to_y(k))
    arrived(gout_ref.at[core, two, 0, pl.ds(0, 3)], 22)
    for k in range(1, xn):
        send(gout_ref.at[core, two, x_at], gout_ref.at[core, two, x_at], 23, to_x(k))

    arrived(a2a_in.at[most], 15)
    half_buf[...] += dot(sel_t[...], a2a_in[...], 1, 0)
    fin[...] = half_buf[...].astype(BF)
    qr = cells // 4
    ours = rows_at(n, qr)
    for k, q in enumerate((mate, across, 3 - n)):
        send(fin.at[rows_at(q, qr)], half_in.at[k], 19, (c, q))

    arrived(bz_recv.at[pl.ds(0, zs - 1)], 16)
    b_all = bz_recv[0]
    for k in range(1, zs):
        b_all += bz_recv[k]
    bout_ref[core] = b_all
    send(bout_ref.at[core], bout_ref.at[core], 18, near)

    arrived(gout_ref.at[core, one, :, pl.ds(0, 3)], 21)
    if xn > 1:
        arrived(gout_ref.at[core, two, pl.ds(0, xn - 1)], 23)
    send(gout_ref.at[core], gout_ref.at[core], 24, near)

    zmost = gz_ref.at[core, :, pl.ds(0, (zs - 1) * zq), :]
    arrived(zmost, 30)
    send(gz_ref.at[core], gz_ref.at[core], 32, near)

    arrived(half_in, 19)
    kept = half_buf[ours, :] + half_in[1].astype(F32)
    swapped = half_in[0].astype(F32) + half_in[2].astype(F32)
    as_x = jnp.where(core == 0, kept, swapped)
    as_g = jnp.where(core == 0, swapped, kept)
    out_ref[0] = (as_x + x_ref[ours, :].astype(F32)).astype(BF)
    out_ref[1] = (as_g + g_ref[ours, :].astype(F32)).astype(BF)
    arrived(bout_ref.at[core], 18)

    left(halo.at[core, most, lanes], 0)
    left(halo.at[core, pl.ds(0, some), relay_lanes], 38)

    @pl.when(relays)
    def _():
        left(halo.at[core, most, relay_lanes], 37)

    left(ids_recv.at[pl.ds(0, 3)], 1)
    left(halo.at[core, :, lanes], 2)
    left(halo.at[core, :, relay_lanes], 39)
    for hb in range(4):
        left(grad_in.at[pl.ds(hb * 3, 3)], 3 + hb)
        left(g_recv.at[hb, pl.ds(0, peers - 1)], 7 + hb)
        left(q_recv.at[hb, pl.ds(0, zs - 1)], 25 + hb)
        left(z_recv.at[hb, pl.ds(0, zs - 1)], 33 + hb)
    left(b_in, 11)
    left(far_in, 12)
    left(near_in, 13)
    left(b_recv.at[pl.ds(0, peers - 1)], 14)
    left(a2a_in.at[most], 15)
    left(bz_recv.at[pl.ds(0, zs - 1)], 16)
    left(r_all.at[pl.ds(0, peers - 1)], 17)
    left(bout_ref.at[core], 18)
    left(r_recv.at[pl.ds(0, peers - 1)], 29)
    left(zmost, 30)
    left(half_in, 19)
    left(gout_ref.at[core, one, :, pl.ds(0, 3)], 21)
    left(gout_ref.at[core, two, 0, pl.ds(0, 3)], 22)
    if xn > 1:
        left(gout_ref.at[core, one, pl.ds(0, xn - 1), 0], 20)
        left(gout_ref.at[core, two, pl.ds(0, xn - 1)], 23)
    arrived(gout_ref.at[core], 24)
    left(gout_ref.at[core], 24)
    arrived(gz_ref.at[core], 32)
    left(gz_ref.at[core], 32)


def finish_kernel(outs_ref, gout_ref, gz_ref, bout_ref, y_ref, x_ref, gin_ref, gnet_ref, gbias_ref, gout_full,
                  gin, gnet, gfull, gbias, sem):
    copies = []

    def put(src, dst):
        copies.append(pltpu.make_async_copy(src, dst, sem.at[len(copies)]))
        copies[-1].start()

    put(outs_ref.at[0], y_ref)
    put(outs_ref.at[1], x_ref)
    for hb in range(4):
        block = slice(hb * 256, hb * 256 + 256)
        for h in range(2):
            cols = slice(hb * 256 + h * 128, hb * 256 + h * 128 + 128)
            gin[:, cols] = gout_ref[h, hb * 2].astype(F32)
            gfull[block, h * 128 : h * 128 + 128] = gout_ref[h, hb * 2 + 1].astype(F32)
            gnet[:, cols] = gz_ref[h, hb].astype(F32)
            gbias[:, cols] = bout_ref[h, hb : hb + 1, :]
        put(gin.at[:, block], gin_ref.at[:, block])
        put(gnet.at[:, block], gnet_ref.at[:, block])
        put(gfull.at[block], gout_full.at[block])
    put(gbias, gbias_ref)
    for copy in copies:
        copy.wait()


def shape(dims, kind):
    return jax.ShapeDtypeStruct(dims, kind)


def local(nc, zs, cell_feat, out_grad, w_in, w_net, bias, w_out, send_idx, pin_net, pin_ref, block_count):
    rows = cell_feat.shape[0]
    slots = send_idx.shape[2]
    outer = nc * slots
    pins = pin_ref.shape[3]
    hidden = w_in.shape[1]
    peers = 2 * nc // zs
    gr = 256 // peers
    zq = 256 // zs
    zz = 4 * zq // peers
    dma = pltpu.SemaphoreType.DMA
    vm = pltpu.VMEM

    outs, gout, gz, bout = pl.pallas_call(
        functools.partial(layer_kernel, nc, zs, slots),
        out_shape=(shape((2, rows // 4, F), BF), shape((2, 8, peers // 4, 4, gr, 128), BF),
                   shape((2, 4, 256, 128), BF), shape((2, 8, 128), F32)),
        in_specs=[HBM] * 5 + [VM] + [HBM] * 4,
        out_specs=(VM,) * 4,
        scratch_shapes=[
            vm((rows, F), BF),
            vm((rows, F), BF),
            vm((slots, nc), I32),
            vm((2, pins), I32),
            vm((2, pins), I32),
            vm((1, hidden), F32),
            vm((F, hidden), BF),
            vm((F, hidden), BF),
            vm((hidden, F), BF),
            vm((outer, F), BF),
            vm((2, outer, F), BF),
            vm((8, pins), I32),
            vm((4, 8, pins), I32),
            vm((rows, outer), BF),
            vm((2, pins, rows + outer), BF),
            vm((rows + outer, 2 * pins), BF),
            vm((2, 2, pins, F), BF),
            vm((2, F, pins), BF),
            vm((2, NETS, pins), BF),
            vm((2, pins, NETS), BF),
            vm((2, NETS, F), BF),
            vm((2, F, NETS), BF),
            vm((2, NETS, F), F32),
            vm((pins, 5 * HB), BF),
            vm((pins, 5 * HB), BF),
            vm((NETS, 5 * HB), BF),
            vm((2, 2 * pins, F), BF),
            vm((2, 16, 128), F32),
            vm((2, 12, 256, 128), F32),
            vm((12, 256, 128), F32),
            vm((12, 256, 128), BF),
            vm((4, peers, 2, gr, 128), BF),
            vm((16, 128), F32),
            vm((16, 128), BF),
            vm((peers, 16, 128), BF),
            vm((2, outer, F), F32),
            vm((outer, F), F32),
            vm((2, rows, F), F32),
            vm((rows, F), F32),
            vm((outer, F), BF),
            vm((outer, F), BF),
            vm((rows, F), F32),
            vm((3, rows // 4, F), BF),
            vm((rows, F), BF),
            vm((4, 2 * gr, 128), BF),
            vm((4, zs, 2 * gr, 128), BF),
            vm((8, 128), F32),
            vm((zs, 8, 128), F32),
            vm((8, gr, 128), BF),
            vm((4, zs, zq, 128), BF),
            vm((peers, zz, 128), F32),
            vm((peers, zz, 128), F32),
            vm((zz, 128), F32),
            vm((peers, zz, 128), F32),
            vm((4, zq, 128), BF),
            dma((9,)),
            dma((40,)),
            dma((40,)),
        ],
        compiler_params=pltpu.CompilerParams(collective_id=0, has_side_effects=True, vmem_limit_bytes=48 << 20),
        name="layer",
    )(*[
        pltpu.with_memory_space_constraint(v, pltpu.HBM)
        for v in (cell_feat, out_grad, send_idx[0].T, pin_net.reshape(2, pins), pin_ref.reshape(2, pins))
    ], block_count, *[
        pltpu.with_memory_space_constraint(v, pltpu.HBM) for v in (w_in, w_net, bias.reshape(1, hidden), w_out)
    ])

    updated, cell_grad, grad_in, grad_net, grad_bias, grad_out = pl.pallas_call(
        finish_kernel,
        out_shape=(
            shape((rows // 4, F), BF), shape((rows // 4, F), BF), shape((F, hidden), F32),
            shape((F, hidden), F32), shape((1, hidden), F32), shape((hidden, F), F32),
        ),
        in_specs=[VM] * 4,
        out_specs=(ANY,) * 6,
        scratch_shapes=[
            vm((F, hidden), F32), vm((F, hidden), F32), vm((hidden, F), F32), vm((1, hidden), F32), dma((15,)),
        ],
        compiler_params=pltpu.CompilerParams(vmem_limit_bytes=12 << 20),
        name="finish",
    )(outs, gout.reshape(2, 8, 256, 128), gz, bout)
    return (updated, cell_grad, grad_in, grad_net, grad_bias.reshape(hidden), grad_out)


def solution(mesh):
    nc = mesh.shape["cell"]
    placed = (
        P("cell", None), P("cell", None), P(), P(), P(), P(),
        P("cell", None, None), P("cell", "net", None, None), P("cell", "net", None, None), P("cell", "net"),
    )
    return jax.shard_map(
        functools.partial(local, nc, Z_SIZE),
        mesh=mesh,
        in_specs=placed,
        out_specs=(P(("cell", "net"), None), P(("cell", "net"), None), P(), P(), P(), P()),
        check_vma=False,
    )
```
